128 devices in a mesh: box: 128 (over z, y, x, core).
Axes of the slice: x: 4, y: 4, z: 4, core: 2. Of those that a mesh axis runs over, the one named last changes fastest.
Arguments:
- rhs_fine: float32 [512, 512, 512], P('box'), may hold values from -6 to 6
- coef_zero: float32 [512, 512, 512], P('box'), may hold values from 0.5 to 4
- coef_one: float32 [256, 256, 256], P('box'), may hold values from 0.5 to 4
- coef_two: float32 [128, 128, 128], P('box'), may hold values from 0.5 to 4
- coef_three: float32 [64, 64, 64], replicated, may hold values from 0.5 to 4
Outputs:
- smooth_zero: float32 [512, 512, 512], P('box')
- smooth_one: float32 [256, 256, 256], P('box')
- smooth_two: float32 [128, 128, 128], P('box')
- coarse_solution: float32 [64, 64, 64], replicated
The draws below stay inside these ranges and needn't reach their ends.
All inputs are finite; a program needn't handle non-finite values.
Results may differ from the reference program's by a relative error of at most 0.00002.
Values sent between devices are 32-bit elements; how exact they have to be, the bound alone decides.
No kernel may reach another device: no remote copies, remote signals or barrier semaphores. Data moves between devices by JAX's collectives and lax.ppermute only.
A program may use at most 192 MiB of HBM per device.

```python
import math
import jax
import jax.numpy as jnp
from jax import lax

G = 512
CHEB = 16
NX0 = 512
NX1 = 256
NX2 = 128
NX3 = 64
G1 = 256
G2 = 128
G3 = 64


def block_levels(key, shape, shards, smallest, top_value):
    def one(axis_at, parts):
        draws = jax.random.uniform(jax.random.fold_in(jax.random.fold_in(key, 6), axis_at), (parts,), jnp.float32, smallest / len(shards), top_value / len(shards))
        return jnp.repeat(jnp.exp(draws), shape[axis_at] // parts).reshape((-1,) + (1,) * (len(shape) - axis_at - 1))

    factor_of = one(*shards[0])
    for cut in shards[1:]:
        factor_of = factor_of * one(*cut)
    return factor_of


def gaussian(stream_key, dims, spread, limit, split=(), dtype=jnp.bfloat16):
    factor_of = block_levels(stream_key, dims, split, -0.22, 0.18) if split else 1.0
    entries = jax.random.normal(stream_key, dims, jnp.float32) * spread * factor_of
    return jnp.minimum(jnp.maximum(entries, -limit), limit).astype(dtype)


def setup_inputs(seed: int = 0) -> dict:
    arg_keys = jax.random.split(jax.random.key(seed), 6)
    return {
        "rhs_fine": gaussian(arg_keys[0], (NX0, G, G), 1.0, 6.0, ((0, 128),), jnp.float32),
        "coef_zero": jnp.clip(jnp.exp(math.log(4.0) - 2.0794415 * jax.random.uniform(arg_keys[1], (NX0, G, G), jnp.float32) ** block_levels(arg_keys[1], (NX0, G, G), ((0, 128),), -0.2, 0.2)), 0.5, 4.0),
        "coef_one": jnp.clip(jnp.exp(math.log(4.0) - 2.0794415 * jax.random.uniform(arg_keys[2], (NX1, G1, G1), jnp.float32) ** block_levels(arg_keys[2], (NX1, G1, G1), ((0, 128),), -0.2, 0.2)), 0.5, 4.0),
        "coef_two": jnp.clip(jnp.exp(math.log(4.0) - 2.0794415 * jax.random.uniform(arg_keys[3], (NX2, G2, G2), jnp.float32) ** block_levels(arg_keys[3], (NX2, G2, G2), ((0, 128),), -0.2, 0.2)), 0.5, 4.0),
        "coef_three": jnp.clip(jnp.exp(jax.random.uniform(arg_keys[4], (NX3, G3, G3), jnp.float32, math.log(0.5), math.log(4.0))), 0.5, 4.0),
    }


OMEGA = 0.8
CENTER_VALUE = 1.04
HALF_WIDTH = 0.96


def pad_sides(field):
    return jnp.pad(field, ((0, 0), (1, 1), (1, 1)))


def pad_first(field):
    return jnp.pad(field, ((1, 1), (0, 0), (0, 0)))


def shifted(field, delta_x, delta_y, delta_z):
    return field[1 + delta_x:field.shape[0] - 1 + delta_x, 1 + delta_y:field.shape[1] - 1 + delta_y, 1 + delta_z:field.shape[2] - 1 + delta_z]


OFFSETS = ((1, 0, 0), (-1, 0, 0), (0, 1, 0), (0, -1, 0), (0, 0, 1), (0, 0, -1))


def face_sum(coef_ext):
    padded = pad_sides(coef_ext)
    centre_coef = shifted(padded, 0, 0, 0)
    total = jnp.zeros_like(centre_coef)
    for offset in OFFSETS:
        total = total + 0.5 * (centre_coef + shifted(padded, *offset))
    return total


def apply_operator(field_ext, coef_ext, diagonal):
    padded_coef = pad_sides(coef_ext)
    padded_field = pad_sides(field_ext)
    centre_coef = shifted(padded_coef, 0, 0, 0)
    beside = jnp.zeros_like(centre_coef)
    for offset in OFFSETS:
        beside = beside + 0.5 * (centre_coef + shifted(padded_coef, *offset)) * shifted(padded_field, *offset)
    return diagonal * shifted(padded_field, 0, 0, 0) - beside


def restrict_axis(padded, axis, count):
    return (0.25 * lax.slice_in_dim(padded, 0, count, 2, axis)
            + 0.5 * lax.slice_in_dim(padded, 1, count + 1, 2, axis)
            + 0.25 * lax.slice_in_dim(padded, 2, count + 1, 2, axis))


def restrict_sides(field):
    for axis in (1, 2):
        count = field.shape[axis]
        front = [(0, 0), (0, 0), (0, 0)]
        front[axis] = (1, 0)
        field = restrict_axis(jnp.pad(field, tuple(front)), axis, count)
    return field


def restrict_whole(residual):
    count = residual.shape[0]
    lowered = restrict_axis(jnp.pad(residual, ((1, 0), (0, 0), (0, 0))), 0, count)
    return 4.0 * restrict_sides(lowered)


def chebyshev(rhs_coarse, coef_coarse, iterations):
    coef_ext = pad_first(coef_coarse)
    diagonal = face_sum(coef_ext)
    sigma = CENTER_VALUE / HALF_WIDTH
    step_field = rhs_coarse / (CENTER_VALUE * diagonal)
    iterate = step_field
    remains = rhs_coarse - apply_operator(pad_first(step_field), coef_ext, diagonal)
    rho_start = jnp.float32(1.0 / sigma)

    def advance(index, carry):
        iterate, remains, step_field, rho_now = carry
        rho_new = 1.0 / (2.0 * sigma - rho_now)
        step_field = rho_new * rho_now * step_field + (2.0 * rho_new / HALF_WIDTH) * remains / diagonal
        iterate = iterate + step_field
        remains = remains - apply_operator(pad_first(step_field), coef_ext, diagonal)
        return iterate, remains, step_field, rho_new

    result = lax.fori_loop(0, iterations - 1, advance, (iterate, remains, step_field, rho_start))
    return result[0]


def reference(rhs_fine, coef_zero, coef_one, coef_two, coef_three):
    rhs_level = rhs_fine
    smoothed_all = []
    for coef_level in (coef_zero, coef_one, coef_two):
        coef_ext = pad_first(coef_level)
        diagonal = face_sum(coef_ext)
        first_iter = OMEGA * rhs_level / diagonal
        smoothed = first_iter + OMEGA * (rhs_level - apply_operator(pad_first(first_iter), coef_ext, diagonal)) / diagonal
        residual = rhs_level - apply_operator(pad_first(smoothed), coef_ext, diagonal)
        smoothed_all.append(smoothed)
        rhs_level = restrict_whole(residual)
    coarse_solution = chebyshev(rhs_level, coef_three, CHEB)
    return smoothed_all[0], smoothed_all[1], smoothed_all[2], coarse_solution
```

```python
import jax
import jax.numpy as jnp
import numpy as np
from jax import lax
from jax.experimental import pallas as pl
from jax.experimental.pallas import tpu as pltpu
from jax.sharding import PartitionSpec as P

CHEB = 16
OMEGA = 0.8
CENTER_VALUE = 1.04
HALF_WIDTH = 0.96
ROWS = 8
PAD = 8
LANES = 128
F32 = jnp.float32
BF16 = jnp.bfloat16


def restriction_matrix(fine, coarse_lanes, shift):
    weights = np.zeros((fine, coarse_lanes), np.float32)
    for k in range(fine // 2):
        weights[2 * k, k + shift] = 0.5
        weights[2 * k + 1, k + shift] = 0.25
        if k > 0:
            weights[2 * k - 1, k + shift] = 0.25
    return weights


def shape(*dims):
    return jax.ShapeDtypeStruct(dims, F32)


def call(body, outs, scratch, copies, flops, moved, megabytes, aliases=None):
    sems = [pltpu.SemaphoreType.DMA((copies,))]

    def run(scalars, *arrays):
        return pl.pallas_call(
            body,
            out_shape=outs,
            in_specs=[pl.BlockSpec(memory_space=pltpu.SMEM)]
            + [pl.BlockSpec(memory_space=pl.ANY)] * len(arrays),
            out_specs=[pl.BlockSpec(memory_space=pl.ANY)] * len(outs),
            scratch_shapes=scratch + sems,
            input_output_aliases=aliases or {},
            compiler_params=pltpu.CompilerParams(vmem_limit_bytes=megabytes << 20),
            cost_estimate=pl.CostEstimate(flops=flops, bytes_accessed=moved, transcendentals=0),
        )(scalars, *arrays)

    return run


class Copies:
    def __init__(self, sems):
        self.sems = sems
        self.used = 0

    def start(self, source, target):
        copy = pltpu.make_async_copy(source, target, self.sems.at[self.used])
        self.used += 1
        copy.start()
        return copy

    def choose(self, first_if, source, other, target):
        copy = pltpu.make_async_copy(source, target, self.sems.at[self.used])
        swap = pltpu.make_async_copy(other, target, self.sems.at[self.used])
        self.used += 1

        @pl.when(first_if)
        def _():
            copy.start()

        @pl.when(jnp.logical_not(first_if))
        def _():
            swap.start()

        return copy


def clear_pads(ref, size):
    planes, _, lanes = ref.shape
    zeros = jnp.zeros((planes, PAD, lanes), F32)
    ref[:, :PAD, :] = zeros
    ref[:, PAD + size :, :] = zeros


def inner(ref, plane, size):
    return ref.at[plane, pl.ds(PAD, size), :]


def at_rows(ref, plane, row, offset=0):
    return ref[plane, pl.ds(PAD + row + offset, ROWS), :]


def in_plane(ref, plane, row):
    centre = at_rows(ref, plane, row)
    lanes = centre.shape[1]
    lane = lax.broadcasted_iota(jnp.int32, centre.shape, 1)
    left = jnp.where(lane == 0, 0.0, pltpu.roll(centre, 1, 1))
    right = jnp.where(lane == lanes - 1, 0.0, pltpu.roll(centre, lanes - 1, 1))
    tall = ref[plane, pl.ds(PAD + row - 8, ROWS + 16), :]
    return centre, [tall[9 : 9 + ROWS], tall[7 : 7 + ROWS], left, right]


def around(ref, plane, row, sides):
    centre, beside = in_plane(ref, plane, row)
    return centre, beside + [at_rows(ref, plane + side, row) for side in sides]


def total(values):
    result = values[0]
    for value in values[1:]:
        result = result + value
    return result


def sweep(size, body):
    def step(index, carry):
        body(pl.multiple_of(index * ROWS, ROWS))
        return carry

    lax.fori_loop(0, size // ROWS, step, 0, unroll=2)


def faces(coef, coef_beside, field_beside):
    return total([(coef + c) * v for c, v in zip(coef_beside, field_beside)])


def put_tiles(tiles, plane, row, value):
    for tile in range(tiles.shape[1]):
        tiles[plane, tile, pl.ds(PAD + row, ROWS), :] = value[:, tile * LANES : (tile + 1) * LANES]


def clear_top(tiles):
    tiles[:, :, :PAD, :] = jnp.zeros((tiles.shape[0], tiles.shape[1], PAD, LANES), F32)


def thin_rows(tiles, plane, start, count):
    parts = []
    for tile in range(tiles.shape[1]):
        parts.append(
            0.25 * tiles[plane, tile, pl.ds(PAD - 1 + start, count, stride=2), :]
            + 0.5 * tiles[plane, tile, pl.ds(PAD + start, count, stride=2), :]
            + 0.25 * tiles[plane, tile, pl.ds(PAD + 1 + start, count, stride=2), :]
        )
    return jnp.concatenate(parts, axis=1)


def restrict_plane(tiles, plane, size, matrix):
    return project(thin_rows(tiles, plane, 0, size // 2), matrix)


def project(rows, matrix):
    high = rows.astype(BF16)
    rest = rows - high.astype(F32)
    middle = rest.astype(BF16)
    low = (rest - middle.astype(F32)).astype(BF16)
    return (
        jnp.dot(low, matrix, preferred_element_type=F32)
        + jnp.dot(middle, matrix, preferred_element_type=F32)
        + jnp.dot(high, matrix, preferred_element_type=F32)
    )


def plane_at(core, place):
    return place + core * (3 - 2 * place)


def first_inner(scalars, coef, rhs, first, partial, c, b, f, g, sems):
    core = scalars[0]
    size = coef.shape[1]
    go = Copies(sems)
    waits = [go.start(coef.at[plane_at(core, q)], inner(c, q, size)) for q in range(4)]
    more = [go.start(rhs.at[plane_at(core, q)], b.at[q - 1]) for q in (1, 2)]
    clear_pads(c, size)
    for copy in waits + more:
        copy.wait()
    out = []
    for slot, q, sides in ((0, 0, (1,)), (1, 3, (-1,))):

        def partial_rows(row):
            centre, beside = around(c, q, row, sides)
            g[slot, pl.ds(row, ROWS), :] = 3.0 * centre + 0.5 * total(beside)

        sweep(size, partial_rows)
        out.append(go.start(g.at[slot], partial.at[slot]))
    for q in (1, 2):

        def first_rows(row):
            centre, beside = around(c, q, row, (-1, 1))
            diagonal = 3.0 * centre + 0.5 * total(beside)
            f[q - 1, pl.ds(row, ROWS), :] = OMEGA * b[q - 1, pl.ds(row, ROWS), :] / diagonal

        sweep(size, first_rows)
        out.append(go.start(f.at[q - 1], first.at[q - 1]))
    for copy in out:
        copy.wait()


def first_rim(scalars, rhs, partial, coef_outer, coef_sibling, outer, sibling, b, g, h, f, sems):
    core = scalars[0]
    size = rhs.shape[1]
    go = Copies(sems)
    loads = []
    for slot, q, halo in ((0, 0, coef_outer), (1, 3, coef_sibling)):
        loads.append(
            [
                go.start(rhs.at[plane_at(core, q)], b.at[slot]),
                go.start(partial.at[slot], g.at[slot]),
                go.start(halo, h.at[slot]),
            ]
        )
    out = []
    for slot, target in ((0, outer), (1, sibling)):
        for copy in loads[slot]:
            copy.wait()

        def rows(row):
            part = pl.ds(row, ROWS)
            diagonal = g[slot, part, :] + 0.5 * h[slot, part, :]
            f[slot, part, :] = OMEGA * b[slot, part, :] / diagonal

        sweep(size, rows)
        out.append(go.start(f.at[slot], target))
    for copy in out:
        copy.wait()


def smooth_inner(
    scalars, coef, rhs, coef_outer, coef_sibling, first, first_outer, first_sibling,
    smooth, known, factor, c, v, b, s, g, h, sems,
):
    core = scalars[0]
    size = coef.shape[1]
    go = Copies(sems)
    c_loads = [go.start(coef_outer, inner(c, 0, size))]
    c_loads += [go.start(coef.at[plane_at(core, q)], inner(c, q + 1, size)) for q in range(4)]
    c_loads.append(go.start(coef_sibling, inner(c, 5, size)))
    sources = (first_outer, first.at[0], first.at[1], first_sibling)
    v_loads = [go.start(source, inner(v, q + 1, size)) for q, source in enumerate(sources)]
    b_loads = [go.start(rhs.at[plane_at(core, q)], b.at[q]) for q in range(4)]
    clear_pads(c, size)
    clear_pads(v, size)
    for copy in c_loads + v_loads + b_loads:
        copy.wait()
    out = []
    for slot, q, side in ((0, 1, 1), (1, 4, -1)):

        def rim_rows(row):
            part = pl.ds(row, ROWS)
            coef_here, coef_beside = around(c, q, row, (side,))
            here, beside = around(v, q, row, (side,))
            halo = at_rows(c, q - side, row)
            diagonal = 3.0 * coef_here + 0.5 * (total(coef_beside) + halo)
            scale = OMEGA / diagonal
            applied = diagonal * here - 0.5 * faces(coef_here, coef_beside, beside)
            g[slot, part, :] = here + scale * (b[q - 1, part, :] - applied)
            h[slot, part, :] = 0.5 * scale * (coef_here + halo)

        sweep(size, rim_rows)
        out.append(go.start(g.at[slot], known.at[slot]))
        out.append(go.start(h.at[slot], factor.at[slot]))
    for q in (2, 3):

        def rows(row):
            part = pl.ds(row, ROWS)
            coef_here, coef_beside = around(c, q, row, (-1, 1))
            here, beside = around(v, q, row, (-1, 1))
            diagonal = 3.0 * coef_here + 0.5 * total(coef_beside)
            applied = diagonal * here - 0.5 * faces(coef_here, coef_beside, beside)
            s[q - 2, part, :] = here + OMEGA * (b[q - 1, part, :] - applied) / diagonal

        sweep(size, rows)
        out.append(go.start(s.at[q - 2], smooth.at[plane_at(core, q - 1)]))
    for copy in out:
        copy.wait()


def smooth_rim(
    scalars, started, known, factor, halo_outer, halo_sibling,
    smooth, outer, sibling, g, h, v, s, sems,
):
    core = scalars[0]
    size = known.shape[1]
    go = Copies(sems)
    loads = []
    for slot, halo in ((0, halo_outer), (1, halo_sibling)):
        loads.append(
            [
                go.start(known.at[slot], g.at[slot]),
                go.start(factor.at[slot], h.at[slot]),
                go.start(halo, v.at[slot]),
            ]
        )
    out = []
    for slot, q, target in ((0, 0, outer), (1, 3, sibling)):
        for copy in loads[slot]:
            copy.wait()

        def rows(row):
            part = pl.ds(row, ROWS)
            s[slot, part, :] = g[slot, part, :] + h[slot, part, :] * v[slot, part, :]

        sweep(size, rows)
        out.append(go.start(s.at[slot], target))
        out.append(go.start(s.at[slot], smooth.at[plane_at(core, q)]))
    for copy in out:
        copy.wait()


def residual_inner(
    scalars, coef, rhs, coef_outer, coef_sibling, smooth, smooth_outer, smooth_sibling, matrix,
    lowered, known, factor, c, v, b, g, h, t, low, mat, sems,
):
    core = scalars[0]
    size = coef.shape[1]
    go = Copies(sems)
    loads = [go.start(coef_outer, inner(c, 0, size))]
    loads += [go.start(coef.at[plane_at(core, q)], inner(c, q + 1, size)) for q in range(4)]
    loads.append(go.start(coef_sibling, inner(c, 5, size)))
    sources = (
        smooth_outer, smooth.at[plane_at(core, 1)], smooth.at[plane_at(core, 2)], smooth_sibling,
    )
    loads += [go.start(source, inner(v, q + 1, size)) for q, source in enumerate(sources)]
    loads += [go.start(rhs.at[plane_at(core, q)], b.at[q]) for q in range(4)]
    loads.append(go.start(matrix, mat))
    clear_pads(c, size)
    clear_pads(v, size)
    clear_top(t)
    for copy in loads:
        copy.wait()
    out = []
    for slot, q, side in ((0, 1, 1), (1, 4, -1)):

        def rim_rows(row):
            part = pl.ds(row, ROWS)
            coef_here, coef_beside = around(c, q, row, (side,))
            here, beside = around(v, q, row, (side,))
            halo = at_rows(c, q - side, row)
            diagonal = 3.0 * coef_here + 0.5 * (total(coef_beside) + halo)
            applied = diagonal * here - 0.5 * faces(coef_here, coef_beside, beside)
            g[slot, part, :] = b[q - 1, part, :] - applied
            h[slot, part, :] = 0.5 * (coef_here + halo)

        sweep(size, rim_rows)
        out.append(go.start(g.at[slot], known.at[slot]))
        out.append(go.start(h.at[slot], factor.at[slot]))
    for q in (2, 3):

        def rows(row):
            part = pl.ds(row, ROWS)
            coef_here, coef_beside = around(c, q, row, (-1, 1))
            here, beside = around(v, q, row, (-1, 1))
            diagonal = 3.0 * coef_here + 0.5 * total(coef_beside)
            applied = diagonal * here - 0.5 * faces(coef_here, coef_beside, beside)
            put_tiles(t, q - 2, row, b[q - 1, part, :] - applied)

        sweep(size, rows)
        low[q - 2] = restrict_plane(t, q - 2, size, mat[...])
    out.append(go.start(low, lowered))
    for copy in out:
        copy.wait()


def residual_rim(
    scalars, known, factor, halo_outer, halo_sibling, lowered, matrix,
    packed, g, h, v, t, low, pack, mat, sems,
):
    core = scalars[0]
    size = known.shape[1]
    go = Copies(sems)
    loads = []
    for slot, halo in ((0, halo_outer), (1, halo_sibling)):
        loads.append(
            [
                go.start(known.at[slot], g.at[slot]),
                go.start(factor.at[slot], h.at[slot]),
                go.start(halo, v.at[slot]),
            ]
        )
    more = [go.start(lowered, low.at[pl.ds(1, 2)]), go.start(matrix, mat)]
    clear_top(t)
    for copy in more:
        copy.wait()
    for slot in (0, 1):
        for copy in loads[slot]:
            copy.wait()

        def rows(row):
            part = pl.ds(row, ROWS)
            put_tiles(t, slot, row, g[slot, part, :] + h[slot, part, :] * v[slot, part, :])

        sweep(size, rows)
        low[3 * slot] = restrict_plane(t, slot, size, mat[...])
    one = plane_at(core, 1)
    two = plane_at(core, 2)
    last = low[plane_at(core, 3)]
    pack[0] = 2.0 * low[plane_at(core, 0)] + low[one]
    pack[1] = low[one] + 2.0 * low[two] + last
    pack[2] = last
    copy = go.start(pack, packed)
    copy.wait()


def guarded(diagonal):
    return jnp.where(diagonal == 0.0, 1.0, diagonal)


def first_wide(c, b, f, planes, size):
    for q in range(planes):

        def rows(row):
            centre, beside = around(c, q + 1, row, (-1, 1))
            diagonal = guarded(3.0 * centre + 0.5 * total(beside))
            f[q, pl.ds(PAD + row, ROWS), :] = OMEGA * b[q, pl.ds(row, ROWS), :] / diagonal

        sweep(size, rows)


def smooth_wide(c, b, f, s, planes, size, inside):
    for q in range(planes):

        def rows(row):
            coef_here, coef_beside = around(c, q + 2, row, (-1, 1))
            here, beside = around(f, q + 1, row, (-1, 1))
            diagonal = guarded(3.0 * coef_here + 0.5 * total(coef_beside))
            applied = diagonal * here - 0.5 * faces(coef_here, coef_beside, beside)
            value = here + OMEGA * (b[q + 1, pl.ds(row, ROWS), :] - applied) / diagonal
            if inside[q] is not None:
                value = jnp.where(inside[q], value, 0.0)
            s[q, pl.ds(PAD + row, ROWS), :] = value

        sweep(size, rows)


def residual_wide(c, b, s, t, planes, size):
    for q in range(planes):

        def rows(row):
            coef_here, coef_beside = around(c, q + 3, row, (-1, 1))
            here, beside = around(s, q + 1, row, (-1, 1))
            diagonal = 3.0 * coef_here + 0.5 * total(coef_beside)
            applied = diagonal * here - 0.5 * faces(coef_here, coef_beside, beside)
            put_tiles(t, q, row, b[q + 2, pl.ds(row, ROWS), :] - applied)

        sweep(size, rows)


def middle_level(
    scalars, own, sibling, outer, before, coef, coef_sibling, coef_outer, coef_before, coef_after,
    matrix, smooth, packed, m, b, c, f, s, t, pack, mat, sems,
):
    core = scalars[0]
    place = scalars[1]
    final = scalars[2]
    size = coef.shape[1]
    even = core == 0
    go = Copies(sems)
    loads = [
        go.start(own, m.at[pl.ds(3, 3)]),
        go.choose(even, outer, sibling, m.at[pl.ds(0, 3)]),
        go.choose(even, sibling, outer, m.at[pl.ds(6, 3)]),
        go.start(before, m.at[9]),
        go.start(coef_before.at[pl.ds(0, size)], inner(c, 0, size)),
        go.start(coef_after.at[pl.ds(0, size)], inner(c, 7, size)),
        go.start(matrix, mat),
    ]
    for q in range(2):
        part = pl.ds(q * size, size)
        loads.append(go.choose(even, coef_outer.at[part], coef_sibling.at[part], inner(c, 1 + q, size)))
        loads.append(go.start(coef.at[q], inner(c, 3 + q, size)))
        loads.append(go.choose(even, coef_sibling.at[part], coef_outer.at[part], inner(c, 5 + q, size)))
    clear_pads(c, size)
    clear_pads(f, size)
    clear_pads(s, size)
    clear_top(t)
    for copy in loads:
        copy.wait()

    def rows(row):
        part = pl.ds(row, ROWS)
        b[0, part, :] = m[0, part, :] + m[9, part, :]
        b[1, part, :] = m[1, part, :]
        b[2, part, :] = m[3, part, :] + m[2, part, :]
        b[3, part, :] = m[4, part, :]
        b[4, part, :] = jnp.where(place < final, m[6, part, :] + m[5, part, :], 0.0)
        b[5, part, :] = m[7, part, :]

    sweep(size, rows)
    first_wide(c, b, f, 6, size)
    smooth_wide(c, b, f, s, 4, size, (place > 0, None, None, place < final))
    out = [go.start(inner(s, 1 + q, size), smooth.at[q]) for q in range(2)]
    residual_wide(c, b, s, t, 2, size)
    low = restrict_plane(t, 1, size, mat[...])
    pack[0] = 2.0 * restrict_plane(t, 0, size, mat[...]) + low
    pack[1] = low
    out.append(go.start(pack, packed))
    for copy in out:
        copy.wait()


def last_level(
    scalars, own, sibling, outer, before, after, rim, coef, coef_sibling, coef_outer, coef_before,
    coef_after, matrices, smooth, copies, m, b, c, f, s, t, w, mat, sems,
):
    core = scalars[0]
    place = scalars[1]
    final = scalars[2]
    size = coef.shape[1]
    half = size // 2
    base = 4 * size
    even = core == 0
    go = Copies(sems)
    loads = [
        go.start(before, m.at[pl.ds(0, 2)]),
        go.choose(even, outer, sibling, m.at[pl.ds(2, 2)]),
        go.start(own, m.at[pl.ds(4, 2)]),
        go.choose(even, sibling, outer, m.at[pl.ds(6, 2)]),
        go.start(after, m.at[pl.ds(8, 2)]),
        go.start(rim, m.at[10]),
        go.start(coef.at[0], inner(c, 3, size)),
        go.start(matrices, mat),
    ]
    for part in range(2):
        target = pl.ds(PAD + part * half, half)
        lanes = pl.ds(part * size, size)
        outer_part = coef_outer.at[pl.ds(base, half), lanes]
        sibling_part = coef_sibling.at[pl.ds(base, half), lanes]
        loads.append(go.choose(even, outer_part, sibling_part, c.at[2, target, :]))
        loads.append(go.choose(even, sibling_part, outer_part, c.at[4, target, :]))
        for source, nearer, farther in ((coef_before, 1, 0), (coef_after, 5, 6)):
            loads.append(go.start(source.at[pl.ds(2 * size, half), lanes], c.at[nearer, target, :]))
            loads.append(
                go.start(source.at[pl.ds(2 * size + half, half), lanes], c.at[farther, target, :])
            )
    clear_pads(c, size)
    clear_pads(f, size)
    clear_pads(s, size)
    clear_top(t)
    for copy in loads:
        copy.wait()

    def rows(row):
        part = pl.ds(row, ROWS)
        b[0, part, :] = m[0, part, :] + m[10, part, :]
        b[1, part, :] = m[2, part, :] + m[1, part, :]
        b[2, part, :] = m[4, part, :] + m[3, part, :]
        b[3, part, :] = jnp.where(place < final, m[6, part, :] + m[5, part, :], 0.0)
        b[4, part, :] = jnp.where(place < final - 1, m[8, part, :] + m[7, part, :], 0.0)

    sweep(size, rows)
    first_wide(c, b, f, 5, size)
    smooth_wide(c, b, f, s, 3, size, (place > 0, None, place < final))
    out = [go.start(inner(s, 1, size), smooth.at[0])]
    residual_wide(c, b, s, t, 1, size)
    top = thin_rows(t, 0, 0, size // 4)
    bottom = thin_rows(t, 0, half, size // 4)
    result = project(top, mat[0]) + project(bottom, mat[1])
    w[...] = jnp.broadcast_to(result[None], w.shape)
    out.append(go.start(w, copies))
    for copy in out:
        copy.wait()


def coarse_level(scalars, own, sibling, coef, solution, e, o, c, w, p, g, x, y, sems):
    core = scalars[0]
    even = core == 0
    half, size, lanes = coef.shape
    go = Copies(sems)
    loads = [
        go.start(coef, c.at[pl.ds(1, half)]),
        go.choose(even, own, sibling, e),
        go.choose(even, sibling, own, o.at[pl.ds(1, 2 * half)]),
    ]
    o[0] = jnp.zeros(o.shape[1:], F32)
    loads[0].wait()
    lane = lax.broadcasted_iota(jnp.int32, (size, lanes), 1)
    row = lax.broadcasted_iota(jnp.int32, (size, lanes), 0)
    upper = lane >= size
    low_edge = (lane % size) == 0
    high_edge = (lane % size) == size - 1
    c[0] = jnp.where(upper, pltpu.roll(c[half], size, 1), 0.0)
    c[half + 1] = jnp.where(upper, 0.0, pltpu.roll(c[1], size, 1))

    def beside(here):
        return [
            pltpu.roll(here, size - 1, 0), pltpu.roll(here, 1, 0),
            pltpu.roll(here, lanes - 1, 1), pltpu.roll(here, 1, 1),
        ]

    edges = [row == size - 1, row == 0, high_edge, low_edge]

    for copy in loads[1:]:
        copy.wait()
    short = lax.broadcasted_iota(jnp.int32, (size // 2, lanes), 1) >= size

    def prepare(q, carry):
        here = c[q + 1]
        sides = [jnp.where(edge, 0.0, value) for edge, value in zip(edges, beside(here))]
        sides += [c[q], c[q + 2]]
        inverse = 1.0 / (3.0 * here + 0.5 * total(sides))
        scaled = 0.5 * inverse
        for d, side in enumerate(sides):
            weight = (here + side) * scaled
            if d < 4:
                weight = jnp.where(edges[d], 0.0, weight)
            elif d == 4:
                weight = jnp.where(jnp.logical_and(q == 0, jnp.logical_not(upper)), 0.0, weight)
            else:
                weight = jnp.where(jnp.logical_and(q == half - 1, upper), 0.0, weight)
            w[d, q] = weight
        lower_rhs = o[q] + 2.0 * e[q] + o[q + 1]
        upper_rhs = o[q + half] + 2.0 * e[q + half] + o[q + half + 1]
        top = jnp.where(short, pltpu.roll(upper_rhs, size, 1), lower_rhs)
        bottom = jnp.where(short, upper_rhs, pltpu.roll(lower_rhs, size, 1))
        scaled_rhs = jnp.concatenate([top, bottom], axis=0) * inverse
        step = scaled_rhs * (1.0 / CENTER_VALUE)
        g[q] = scaled_rhs
        p[0, q + 1] = step
        x[q] = step
        return carry

    lax.fori_loop(0, half, prepare, 0)
    sigma = CENTER_VALUE / HALF_WIDTH
    rho = 1.0 / sigma
    for index in range(CHEB - 1):
        now, later = index % 2, (index + 1) % 2
        p[now, 0] = pltpu.roll(p[now, half], size, 1)
        p[now, half + 1] = pltpu.roll(p[now, 1], size, 1)
        rho_new = 1.0 / (2.0 * sigma - rho)
        keep = rho_new * rho
        gain = 2.0 * rho_new / HALF_WIDTH
        rho = rho_new
        final = index == CHEB - 2

        def advance(q, carry):
            here = p[now, q + 1]
            sides = beside(here) + [p[now, q], p[now, q + 2]]
            remains = g[q] - here + total([w[d, q] * side for d, side in enumerate(sides)])
            step = keep * here + gain * remains
            value = x[q] + step
            if final:
                y[q] = value[:, :size]
                y[q + half] = pltpu.roll(value, size, 1)[:, :size]
            else:
                g[q] = remains
                p[later, q + 1] = step
                x[q] = value
            return carry

        lax.fori_loop(0, half, advance, 0, unroll=2)
    copy = go.start(y, solution)
    copy.wait()


def vm(*dims):
    return pltpu.VMEM(dims, F32)


def swapped(value, pairs):
    return lax.ppermute(value, "box", pairs)


def local(rhs_fine, coef_zero, coef_one, coef_two, coef_three):
    count = lax.axis_size("box")
    place = lax.axis_index("box")
    core = place % 2
    scalars = jnp.stack([core, place, jnp.int32(count - 1)]).astype(jnp.int32)
    near = [(i, i ^ 1) for i in range(count)]
    far = [(i, i + 1) for i in range(1, count - 1, 2)]
    far = far + [(j, i) for i, j in far]

    def onward(value, distance):
        route = [(i, i + distance) for i in range(count) if 0 <= i + distance < count]
        return lax.ppermute(value, "box", route)

    n = coef_zero.shape[1]
    n1, n2 = n // 2, n // 4
    n3 = n // 8
    plane = n * n * 4
    matrix0 = jnp.asarray(restriction_matrix(n, n1, 0), BF16)
    matrix1 = jnp.asarray(restriction_matrix(n1, n2, 0), BF16)
    both = np.stack([restriction_matrix(n2, 2 * n3, 0), restriction_matrix(n2, 2 * n3, n3)])
    matrix2 = jnp.asarray(both, BF16)

    def side_plane(field, where):
        return lax.dynamic_index_in_dim(field, where, 0, keepdims=False)

    coef_outer = swapped(side_plane(coef_zero, 3 * core), far)
    coef_sibling = swapped(side_plane(coef_zero, 3 - 3 * core), near)
    first, partial = call(
        first_inner, [shape(2, n, n), shape(2, n, n)],
        [vm(4, n + 16, n), vm(2, n, n), vm(2, n, n), vm(2, n, n)], 10, 40 * n * n, 12 * plane, 40,
    )(scalars, coef_zero, rhs_fine)
    first_outer, first_sibling = call(
        first_rim, [shape(n, n), shape(n, n)],
        [vm(2, n, n)] * 4, 8, 10 * n * n, 8 * plane, 40,
    )(scalars, rhs_fine, partial, coef_outer, coef_sibling)

    halo_outer = swapped(first_outer, far)
    halo_sibling = swapped(first_sibling, near)
    smooth, known, factor = call(
        smooth_inner, [shape(4, n, n), shape(2, n, n), shape(2, n, n)],
        [vm(6, n + 16, n), vm(6, n + 16, n), vm(4, n, n), vm(2, n, n), vm(2, n, n), vm(2, n, n)],
        20, 160 * n * n, 20 * plane, 48,
    )(scalars, coef_zero, rhs_fine, coef_outer, coef_sibling, first, first_outer, first_sibling)
    smooth_zero, smooth_outer, smooth_sibling = call(
        smooth_rim, [shape(4, n, n), shape(n, n), shape(n, n)],
        [vm(2, n, n)] * 4, 10, 4 * n * n, 10 * plane, 40, {1: 0},
    )(scalars, smooth, known, factor, halo_outer, halo_sibling)

    halo_outer = swapped(smooth_outer, far)
    halo_sibling = swapped(smooth_sibling, near)

    def folded(field):
        return jnp.concatenate([field[: n2 // 2], field[n2 // 2 :]], axis=1)

    own_two = folded(coef_two[0])
    coefs = jnp.concatenate([coef_one[0], coef_one[1], own_two], axis=0)
    coefs_sibling = swapped(coefs, near)
    coefs_outer = swapped(coefs, far)
    left_two = jnp.where(core == 0, coefs_outer[2 * n1 :], coefs_sibling[2 * n1 :])
    right_two = jnp.where(core == 0, coefs_sibling[2 * n1 :], coefs_outer[2 * n1 :])
    coefs_before = onward(jnp.concatenate([coef_one[1], own_two, left_two], axis=0), 2)
    coefs_after = onward(jnp.concatenate([coef_one[0], own_two, right_two], axis=0), -2)

    lowered, known, factor = call(
        residual_inner, [shape(2, n1, n1), shape(2, n, n), shape(2, n, n)],
        [vm(6, n + 16, n), vm(6, n + 16, n), vm(4, n, n), vm(2, n, n), vm(2, n, n),
         vm(2, n // LANES, n + 16, LANES), vm(2, n1, n1), pltpu.VMEM((n, n1), BF16)],
        20, 160 * n * n, 20 * plane, 48,
    )(scalars, coef_zero, rhs_fine, coef_outer, coef_sibling, smooth_zero, smooth_outer,
      smooth_sibling, matrix0)
    (packed,) = call(
        residual_rim, [shape(3, n1, n1)],
        [vm(2, n, n), vm(2, n, n), vm(2, n, n), vm(2, n // LANES, n + 16, LANES), vm(4, n1, n1), vm(3, n1, n1),
         pltpu.VMEM((n, n1), BF16)],
        10, 20 * n * n, 8 * plane, 40,
    )(scalars, known, factor, halo_outer, halo_sibling, lowered, matrix0)

    packed_outer = swapped(packed, far)
    packed_before = onward(packed[2], 2)
    packed_sibling = swapped(packed, near)
    smooth_one, packed = call(
        middle_level, [shape(2, n1, n1), shape(2, n2, n2)],
        [vm(10, n1, n1), vm(6, n1, n1), vm(8, n1 + 16, n1), vm(6, n1 + 16, n1),
         vm(4, n1 + 16, n1), vm(2, n1 // LANES, n1 + 16, LANES), vm(2, n2, n2), pltpu.VMEM((n1, n2), BF16)],
        18, 400 * n1 * n1, 24 * n1 * n1 * 4, 40,
    )(scalars, packed, packed_sibling, packed_outer, packed_before, coef_one, coefs_sibling,
      coefs_outer, coefs_before, coefs_after, matrix1)

    packed_outer = swapped(packed, far)
    packed_before = onward(packed, 2)
    packed_after = onward(packed, -2)
    packed_rim = onward(packed[1], 3)
    packed_sibling = swapped(packed, near)
    groups = [[i for i in range(count) if i % 2 == r] for r in range(2)]
    smooth_two, copies = call(
        last_level, [shape(1, n2, n2), shape(count // 2, n3 // 2, 2 * n3)],
        [vm(11, n2, n2), vm(5, n2, n2), vm(7, n2 + 16, n2), vm(5, n2 + 16, n2),
         vm(3, n2 + 16, n2), vm(1, n2 // LANES, n2 + 16, LANES), vm(count // 2, n3 // 2, 2 * n3),
         pltpu.VMEM((2, n2, 2 * n3), BF16)],
        24, 300 * n2 * n2, 40 * n2 * n2 * 4, 40,
    )(scalars, packed, packed_sibling, packed_outer, packed_before, packed_after, packed_rim,
      coef_two, coefs_sibling, coefs_outer, coefs_before, coefs_after, matrix2)

    gathered = lax.all_to_all(copies, "box", 0, 0, tiled=True, axis_index_groups=groups)
    gathered_sibling = swapped(gathered, near)
    half = n3 // 2
    coef_pair = jnp.concatenate([coef_three[:half], coef_three[half:]], axis=2)
    (coarse_solution,) = call(
        coarse_level, [shape(n3, n3, n3)],
        [vm(n3, half, 2 * n3), vm(n3 + 1, half, 2 * n3), vm(half + 2, n3, 2 * n3),
         vm(6, half, n3, 2 * n3), vm(2, half + 2, n3, 2 * n3), vm(half, n3, 2 * n3),
         vm(half, n3, 2 * n3), vm(n3, n3, n3)],
        4, 300 * n3 * n3 * n3, 20 * n3 * n3 * n3, 48,
    )(scalars, gathered, gathered_sibling, coef_pair)
    return (smooth_zero, smooth_one, smooth_two, coarse_solution)


def solution(mesh):
    placed = (
        P("box", None, None),
        P("box", None, None),
        P("box", None, None),
        P("box", None, None),
        P(),
    )
    return jax.shard_map(
        local,
        mesh=mesh,
        in_specs=placed,
        out_specs=(P("box", None, None), P("box", None, None), P("box", None, None), P()),
        check_vma=False,
    )
```

```python
import jax
import jax.numpy as jnp
import numpy as np
from jax import lax
from jax.experimental import pallas as pl
from jax.experimental.pallas import tpu as pltpu
from jax.sharding import PartitionSpec as P

CHEB = 16
OMEGA = 0.8
CENTER_VALUE = 1.04
HALF_WIDTH = 0.96
ROWS = 8
UNROLL = 16
PAD = 8
LANES = 128
F32 = jnp.float32
BF16 = jnp.bfloat16


def restriction_matrix(fine, coarse_lanes, shift):
    weights = np.zeros((fine, coarse_lanes), np.float32)
    for k in range(fine // 2):
        weights[2 * k, k + shift] = 0.5
        weights[2 * k + 1, k + shift] = 0.25
        if k > 0:
            weights[2 * k - 1, k + shift] = 0.25
    return weights


def shape(*dims):
    return jax.ShapeDtypeStruct(dims, F32)


def call(body, outs, scratch, copies, flops, moved, megabytes, aliases=None):
    sems = [pltpu.SemaphoreType.DMA((copies,))]

    def run(scalars, *arrays):
        return pl.pallas_call(
            body,
            out_shape=outs,
            in_specs=[pl.BlockSpec(memory_space=pltpu.SMEM)]
            + [pl.BlockSpec(memory_space=pl.ANY)] * len(arrays),
            out_specs=[pl.BlockSpec(memory_space=pl.ANY)] * len(outs),
            scratch_shapes=scratch + sems,
            input_output_aliases=aliases or {},
            compiler_params=pltpu.CompilerParams(vmem_limit_bytes=megabytes << 20),
            cost_estimate=pl.CostEstimate(flops=flops, bytes_accessed=moved, transcendentals=0),
        )(scalars, *arrays)

    return run


class Group:
    def __init__(self, copies):
        self.copies = list(copies)

    def wait(self):
        for copy in self.copies:
            copy.wait()


class Copies:
    def __init__(self, sems):
        self.sems = sems
        self.used = 0

    def start(self, source, target):
        copy = pltpu.make_async_copy(source, target, self.sems.at[self.used])
        self.used += 1
        copy.start()
        return copy

    def tiles(self, source, target, rows=None):
        rows = source.shape[0] if rows is None else rows
        return Group(
            self.start(source.at[:, columns(t)], target.at[t, pl.ds(PAD, rows), :])
            for t in range(source.shape[1] // LANES)
        )

    def untiled(self, source, target):
        rows = target.shape[0]
        return Group(
            self.start(source.at[t, pl.ds(PAD, rows), :], target.at[:, columns(t)])
            for t in range(target.shape[1] // LANES)
        )

    def choose(self, first_if, source, other, target):
        copy = pltpu.make_async_copy(source, target, self.sems.at[self.used])
        swap = pltpu.make_async_copy(other, target, self.sems.at[self.used])
        self.used += 1

        @pl.when(first_if)
        def _():
            copy.start()

        @pl.when(jnp.logical_not(first_if))
        def _():
            swap.start()

        return copy


def clear_pads(tiles, size):
    zeros = jnp.zeros(tiles.shape[:2] + (PAD, LANES), F32)
    tiles[:, :, :PAD, :] = zeros
    tiles[:, :, PAD + size :, :] = zeros


def clear_top(tiles):
    tiles[:, :, :PAD, :] = jnp.zeros(tiles.shape[:2] + (PAD, LANES), F32)


def columns(tile):
    return pl.ds(tile * LANES, LANES)


def load_rows(ref, plane, row, offset=0):
    return [ref[plane, t, pl.ds(PAD + row + offset, ROWS), :] for t in range(ref.shape[1])]


def load_flat(ref, plane, row):
    part = pl.ds(row, ROWS)
    return [ref[plane, part, columns(t)] for t in range(ref.shape[2] // LANES)]


def store_rows(ref, plane, row, values):
    for t, value in enumerate(values):
        ref[plane, t, pl.ds(PAD + row, ROWS), :] = value


def store_flat(ref, plane, row, values):
    for t, value in enumerate(values):
        ref[plane, pl.ds(row, ROWS), columns(t)] = value


def store_whole(ref, plane, row, value):
    ref[plane, pl.ds(row, ROWS), :] = value


def each(function, *lists):
    return [function(*values) for values in zip(*lists)]


def lane_sides(centre):
    lane = lax.broadcasted_iota(jnp.int32, (ROWS, LANES), 1)
    first = lane == 0
    last = lane == LANES - 1
    up = [pltpu.roll(value, 1, 1) for value in centre]
    down = [pltpu.roll(value, LANES - 1, 1) for value in centre]
    left = [jnp.where(first, up[t - 1] if t else 0.0, up[t]) for t in range(len(centre))]
    right = [
        jnp.where(last, down[t + 1] if t + 1 < len(centre) else 0.0, down[t])
        for t in range(len(centre))
    ]
    return [left, right]


def around(ref, plane, row, sides):
    centre = load_rows(ref, plane, row)
    beside = lane_sides(centre)
    beside += [load_rows(ref, plane, row, 1), load_rows(ref, plane, row, -1)]
    beside += [load_rows(ref, plane + side, row) for side in sides]
    return centre, beside


def face_totals(coef, beside):
    result = each(lambda c, s: c + s, coef, beside[0])
    for side in beside[1:]:
        result = each(lambda r, c, s: r + (c + s), result, coef, side)
    return result


def stencil(coefs, fields, row, coef_plane, field_plane, sides):
    coef, coef_beside = around(coefs, coef_plane, row, sides)
    here, beside = around(fields, field_plane, row, sides)
    weights = [each(lambda c, s: c + s, coef, side) for side in coef_beside]
    twice = weights[0]
    gathered = each(lambda w, v: w * v, weights[0], beside[0])
    for weight, side in zip(weights[1:], beside[1:]):
        twice = each(lambda a, b: a + b, twice, weight)
        gathered = each(lambda a, w, v: a + w * v, gathered, weight, side)
    return twice, gathered, here, coef


def first_of(rhs, twice):
    return each(lambda b, d: (2.0 * OMEGA) * b / d, rhs, twice)


def smoothed_of(rhs, twice, gathered, here):
    return each(
        lambda b, d, g, v: (1.0 - OMEGA) * v + ((2.0 * OMEGA) * b + OMEGA * g) / d,
        rhs, twice, gathered, here,
    )


def residual_of(rhs, twice, gathered, here):
    return each(lambda b, d, g, v: b - 0.5 * (d * v - g), rhs, twice, gathered, here)


def total(values):
    result = values[0]
    for value in values[1:]:
        result = result + value
    return result


def sweep(size, body):
    def step(index, carry):
        for store, ref, plane, row, values in body(pl.multiple_of(index * ROWS, ROWS)):
            store(ref, plane, row, values)
        return carry

    lax.fori_loop(0, size // ROWS, step, 0, unroll=UNROLL)


def thin_rows(tiles, plane, start, count):
    parts = []
    for tile in range(tiles.shape[1]):
        parts.append(
            0.25 * tiles[plane, tile, pl.ds(PAD - 1 + start, count, stride=2), :]
            + 0.5 * tiles[plane, tile, pl.ds(PAD + start, count, stride=2), :]
            + 0.25 * tiles[plane, tile, pl.ds(PAD + 1 + start, count, stride=2), :]
        )
    return jnp.concatenate(parts, axis=1)


def restrict_plane(tiles, plane, size, matrix):
    return project(thin_rows(tiles, plane, 0, size // 2), matrix)


def project(rows, matrix):
    high = rows.astype(BF16)
    rest = rows - high.astype(F32)
    middle = rest.astype(BF16)
    low = (rest - middle.astype(F32)).astype(BF16)
    return (
        jnp.dot(low, matrix, preferred_element_type=F32)
        + jnp.dot(middle, matrix, preferred_element_type=F32)
        + jnp.dot(high, matrix, preferred_element_type=F32)
    )


def plane_at(core, place):
    return place + core * (3 - 2 * place)


def first_inner(scalars, coef, rhs, first, partial, c, b, f, g, sems):
    core = scalars[0]
    size = coef.shape[1]
    go = Copies(sems)
    waits = [go.tiles(coef.at[plane_at(core, q)], c.at[q]) for q in (0, 1)]
    later = [[go.tiles(coef.at[plane_at(core, 2)], c.at[2])]]
    later[0].append(go.start(rhs.at[plane_at(core, 1)], b.at[0]))
    later.append([go.tiles(coef.at[plane_at(core, 3)], c.at[3])])
    later[1].append(go.start(rhs.at[plane_at(core, 2)], b.at[1]))
    clear_pads(c, size)
    for copy in waits:
        copy.wait()
    out = []

    def partial_plane(slot, q, side):
        def rows(row):
            coef_here, beside = around(c, q, row, (side,))
            twice = face_totals(coef_here, beside)
            return [(store_flat, g, slot, row, each(lambda d, v: d + v, twice, coef_here))]

        sweep(size, rows)
        out.append(go.start(g.at[slot], partial.at[slot]))

    def first_plane(q):
        def rows(row):
            twice = face_totals(*around(c, q, row, (-1, 1)))
            return [(store_flat, f, q - 1, row, first_of(load_flat(b, q - 1, row), twice))]

        sweep(size, rows)
        out.append(go.start(f.at[q - 1], first.at[q - 1]))

    partial_plane(0, 0, 1)
    for copy in later[0]:
        copy.wait()
    first_plane(1)
    for copy in later[1]:
        copy.wait()
    first_plane(2)
    partial_plane(1, 3, -1)
    for copy in out:
        copy.wait()


def first_rim(scalars, rhs, partial, coef_outer, coef_sibling, outer, sibling, b, g, h, f, sems):
    core = scalars[0]
    size = rhs.shape[1]
    go = Copies(sems)
    loads = []
    for slot, q, halo in ((0, 0, coef_outer), (1, 3, coef_sibling)):
        loads.append(
            [
                go.start(rhs.at[plane_at(core, q)], b.at[slot]),
                go.start(partial.at[slot], g.at[slot]),
                go.start(halo, h.at[slot]),
            ]
        )
    out = []
    for slot, target in ((0, outer), (1, sibling)):
        for copy in loads[slot]:
            copy.wait()

        def rows(row):
            twice = each(lambda g, h: g + h, load_flat(g, slot, row), load_flat(h, slot, row))
            return [(store_flat, f, slot, row, first_of(load_flat(b, slot, row), twice))]

        sweep(size, rows)
        out.append(go.start(f.at[slot], target))
    for copy in out:
        copy.wait()


def loads_in_order(go, core, coef, rhs, coef_outer, coef_sibling, sources, c, v, b):
    def coef_in(q):
        if q == 0:
            return go.tiles(coef_outer, c.at[0])
        if q == 5:
            return go.tiles(coef_sibling, c.at[5])
        return go.tiles(coef.at[plane_at(core, q - 1)], c.at[q])

    def field_in(q):
        return go.tiles(sources[q - 1], v.at[q])

    def rhs_in(q):
        return go.start(rhs.at[plane_at(core, q - 1)], b.at[q - 1])

    waits = [[coef_in(0), coef_in(1), coef_in(2), field_in(1), field_in(2), rhs_in(1)]]
    waits.append([coef_in(3), field_in(3), rhs_in(2)])
    waits.append([coef_in(4), field_in(4), rhs_in(3)])
    waits.append([coef_in(5), rhs_in(4)])
    return waits


def smooth_inner(
    scalars, coef, rhs, coef_outer, coef_sibling, first, first_outer, first_sibling,
    smooth, known, factor, c, v, b, s, g, h, sems,
):
    core = scalars[0]
    size = coef.shape[1]
    go = Copies(sems)
    sources = (first_outer, first.at[0], first.at[1], first_sibling)
    waits = loads_in_order(go, core, coef, rhs, coef_outer, coef_sibling, sources, c, v, b)
    clear_pads(c, size)
    clear_pads(v, size)
    out = []

    def rim(slot, q, side):
        def rows(row):
            twice, gathered, here, coef_here = stencil(c, v, row, q, q, (side,))
            edge = each(lambda c, h: c + h, coef_here, load_rows(c, q - side, row))
            twice = each(lambda d, e: d + e, twice, edge)
            scale = [1.0 / value for value in twice]
            known_rows = each(
                lambda b, d, g, v: (1.0 - OMEGA) * v + ((2.0 * OMEGA) * b + OMEGA * g) * d,
                load_flat(b, q - 1, row), scale, gathered, here,
            )
            factor_rows = each(lambda d, e: (OMEGA * e) * d, scale, edge)
            return [(store_flat, g, slot, row, known_rows), (store_flat, h, slot, row, factor_rows)]

        sweep(size, rows)
        out.append(go.start(g.at[slot], known.at[slot]))
        out.append(go.start(h.at[slot], factor.at[slot]))

    def middle(q):
        def rows(row):
            twice, gathered, here, _ = stencil(c, v, row, q, q, (-1, 1))
            values = smoothed_of(load_flat(b, q - 1, row), twice, gathered, here)
            return [(store_flat, s, q - 2, row, values)]

        sweep(size, rows)
        out.append(go.start(s.at[q - 2], smooth.at[plane_at(core, q - 1)]))

    steps = ((rim, (0, 1, 1)), (middle, (2,)), (middle, (3,)), (rim, (1, 4, -1)))
    for needed, (work, arguments) in zip(waits, steps):
        for copy in needed:
            copy.wait()
        work(*arguments)
    for copy in out:
        copy.wait()


def smooth_rim(
    scalars, started, known, factor, halo_outer, halo_sibling,
    smooth, outer, sibling, g, h, v, s, sems,
):
    core = scalars[0]
    size = known.shape[1]
    go = Copies(sems)
    loads = []
    for slot, halo in ((0, halo_outer), (1, halo_sibling)):
        loads.append(
            [
                go.start(known.at[slot], g.at[slot]),
                go.start(factor.at[slot], h.at[slot]),
                go.start(halo, v.at[slot]),
            ]
        )
    out = []
    for slot, q, target in ((0, 0, outer), (1, 3, sibling)):
        for copy in loads[slot]:
            copy.wait()

        def rows(row):
            flat = [load_flat(ref, slot, row) for ref in (g, h, v)]
            return [(store_flat, s, slot, row, each(lambda g, h, v: g + h * v, *flat))]

        sweep(size, rows)
        out.append(go.start(s.at[slot], target))
        out.append(go.start(s.at[slot], smooth.at[plane_at(core, q)]))
    for copy in out:
        copy.wait()


def residual_inner(
    scalars, coef, rhs, coef_outer, coef_sibling, smooth, smooth_outer, smooth_sibling, matrix,
    lowered, known, factor, c, v, b, g, h, t, low, mat, sems,
):
    core = scalars[0]
    size = coef.shape[1]
    go = Copies(sems)
    sources = (
        smooth_outer, smooth.at[plane_at(core, 1)], smooth.at[plane_at(core, 2)], smooth_sibling,
    )
    waits = loads_in_order(go, core, coef, rhs, coef_outer, coef_sibling, sources, c, v, b)
    waits[0].append(go.start(matrix, mat))
    clear_pads(c, size)
    clear_pads(v, size)
    clear_top(t)
    out = []

    def rim(slot, q, side):
        def rows(row):
            twice, gathered, here, coef_here = stencil(c, v, row, q, q, (side,))
            edge = each(lambda c, h: c + h, coef_here, load_rows(c, q - side, row))
            twice = each(lambda d, e: d + e, twice, edge)
            known_rows = residual_of(load_flat(b, q - 1, row), twice, gathered, here)
            factor_rows = [0.5 * value for value in edge]
            return [(store_flat, g, slot, row, known_rows), (store_flat, h, slot, row, factor_rows)]

        sweep(size, rows)
        out.append(go.start(g.at[slot], known.at[slot]))
        out.append(go.start(h.at[slot], factor.at[slot]))

    def middle(q):
        def rows(row):
            twice, gathered, here, _ = stencil(c, v, row, q, q, (-1, 1))
            values = residual_of(load_flat(b, q - 1, row), twice, gathered, here)
            return [(store_rows, t, q - 2, row, values)]

        sweep(size, rows)
        low[q - 2] = restrict_plane(t, q - 2, size, mat[...])

    steps = ((rim, (0, 1, 1)), (middle, (2,)), (middle, (3,)), (rim, (1, 4, -1)))
    for needed, (work, arguments) in zip(waits, steps):
        for copy in needed:
            copy.wait()
        work(*arguments)
    out.append(go.start(low, lowered))
    for copy in out:
        copy.wait()


def residual_rim(
    scalars, known, factor, halo_outer, halo_sibling, lowered, matrix,
    packed, g, h, v, t, low, pack, mat, sems,
):
    core = scalars[0]
    size = known.shape[1]
    go = Copies(sems)
    loads = []
    for slot, halo in ((0, halo_outer), (1, halo_sibling)):
        loads.append(
            [
                go.start(known.at[slot], g.at[slot]),
                go.start(factor.at[slot], h.at[slot]),
                go.start(halo, v.at[slot]),
            ]
        )
    more = [go.start(lowered, low.at[pl.ds(1, 2)]), go.start(matrix, mat)]
    clear_top(t)
    for copy in more:
        copy.wait()
    for slot in (0, 1):
        for copy in loads[slot]:
            copy.wait()

        def rows(row):
            flat = [load_flat(ref, slot, row) for ref in (g, h, v)]
            return [(store_rows, t, slot, row, each(lambda g, h, v: g + h * v, *flat))]

        sweep(size, rows)
        low[3 * slot] = restrict_plane(t, slot, size, mat[...])
    one = plane_at(core, 1)
    two = plane_at(core, 2)
    last = low[plane_at(core, 3)]
    pack[0] = 2.0 * low[plane_at(core, 0)] + low[one]
    pack[1] = low[one] + 2.0 * low[two] + last
    pack[2] = last
    copy = go.start(pack, packed)
    copy.wait()


def guarded(values):
    return [jnp.where(value == 0.0, 1.0, value) for value in values]


def first_wide(c, b, f, planes, size):
    def plane(q):
        def rows(row):
            twice = guarded(face_totals(*around(c, q + 1, row, (-1, 1))))
            return [(store_rows, f, q, row, first_of(load_flat(b, q, row), twice))]

        sweep(size, rows)

    pl.loop(0, planes)(plane)


def smooth_wide(c, b, f, s, planes, size, inside):
    def plane(q):
        keep = inside(q)

        def rows(row):
            twice, gathered, here, _ = stencil(c, f, row, q + 2, q + 1, (-1, 1))
            values = smoothed_of(load_flat(b, q + 1, row), guarded(twice), gathered, here)
            return [(store_rows, s, q, row, [jnp.where(keep, value, 0.0) for value in values])]

        sweep(size, rows)

    pl.loop(0, planes)(plane)


def residual_wide(c, b, s, t, planes, size):
    for q in range(planes):

        def rows(row):
            twice, gathered, here, _ = stencil(c, s, row, q + 3, q + 1, (-1, 1))
            values = residual_of(load_flat(b, q + 2, row), twice, gathered, here)
            return [(store_rows, t, q, row, values)]

        sweep(size, rows)


def middle_level(
    scalars, own, sibling, outer, before, coef, coef_sibling, coef_outer, coef_before, coef_after,
    matrix, smooth, packed, m, b, c, f, s, t, pack, mat, sems,
):
    core = scalars[0]
    place = scalars[1]
    final = scalars[2]
    size = coef.shape[1]
    even = core == 0
    go = Copies(sems)
    loads = [
        go.start(own, m.at[pl.ds(3, 3)]),
        go.choose(even, outer, sibling, m.at[pl.ds(0, 3)]),
        go.choose(even, sibling, outer, m.at[pl.ds(6, 3)]),
        go.start(before, m.at[9]),
        go.tiles(coef_before.at[pl.ds(0, size)], c.at[0]),
        go.tiles(coef_after.at[pl.ds(0, size)], c.at[7]),
        go.start(matrix, mat),
    ]
    for q in range(2):
        part = pl.ds(q * size, size)
        loads.append(go.tiles(coef.at[q], c.at[3 + q]))
        for tile in range(size // LANES):
            outer_part = coef_outer.at[part, columns(tile)]
            sibling_part = coef_sibling.at[part, columns(tile)]
            left = c.at[1 + q, tile, pl.ds(PAD, size), :]
            right = c.at[5 + q, tile, pl.ds(PAD, size), :]
            loads.append(go.choose(even, outer_part, sibling_part, left))
            loads.append(go.choose(even, sibling_part, outer_part, right))
    clear_pads(c, size)
    clear_pads(f, size)
    clear_pads(s, size)
    clear_top(t)
    for copy in loads:
        copy.wait()

    def rows(row):
        part = pl.ds(row, ROWS)
        values = [
            m[0, part, :] + m[9, part, :],
            m[1, part, :],
            m[3, part, :] + m[2, part, :],
            m[4, part, :],
            jnp.where(place < final, m[6, part, :] + m[5, part, :], 0.0),
            m[7, part, :],
        ]
        return [(store_whole, b, q, row, value) for q, value in enumerate(values)]

    sweep(size, rows)
    first_wide(c, b, f, 6, size)
    lowest = jnp.where(place > 0, 0, 1)
    highest = jnp.where(place < final, 3, 2)
    smooth_wide(c, b, f, s, 4, size, lambda q: jnp.logical_and(q >= lowest, q <= highest))
    out = [go.untiled(s.at[1 + q], smooth.at[q]) for q in range(2)]
    residual_wide(c, b, s, t, 2, size)
    low = restrict_plane(t, 1, size, mat[...])
    pack[0] = 2.0 * restrict_plane(t, 0, size, mat[...]) + low
    pack[1] = low
    out.append(go.start(pack, packed))
    for copy in out:
        copy.wait()


def last_level(
    scalars, own, sibling, outer, before, after, rim, coef, coef_sibling, coef_outer, coef_before,
    coef_after, matrices, smooth, copies, m, b, c, f, s, t, w, mat, sems,
):
    core = scalars[0]
    place = scalars[1]
    final = scalars[2]
    size = coef.shape[1]
    half = size // 2
    base = 4 * size
    even = core == 0
    go = Copies(sems)
    loads = [
        go.start(before, m.at[pl.ds(0, 2)]),
        go.choose(even, outer, sibling, m.at[pl.ds(2, 2)]),
        go.start(own, m.at[pl.ds(4, 2)]),
        go.choose(even, sibling, outer, m.at[pl.ds(6, 2)]),
        go.start(after, m.at[pl.ds(8, 2)]),
        go.start(rim, m.at[10]),
        go.tiles(coef.at[0], c.at[3]),
        go.start(matrices, mat),
    ]
    for part in range(2):
        target = pl.ds(PAD + part * half, half)
        lanes = pl.ds(part * size, size)
        outer_part = coef_outer.at[pl.ds(base, half), lanes]
        sibling_part = coef_sibling.at[pl.ds(base, half), lanes]
        loads.append(go.choose(even, outer_part, sibling_part, c.at[2, 0, target, :]))
        loads.append(go.choose(even, sibling_part, outer_part, c.at[4, 0, target, :]))
        for source, nearer, farther in ((coef_before, 1, 0), (coef_after, 5, 6)):
            loads.append(go.start(source.at[pl.ds(2 * size, half), lanes], c.at[nearer, 0, target, :]))
            loads.append(
                go.start(source.at[pl.ds(2 * size + half, half), lanes], c.at[farther, 0, target, :])
            )
    clear_pads(c, size)
    clear_pads(f, size)
    clear_pads(s, size)
    clear_top(t)
    for copy in loads:
        copy.wait()

    def rows(row):
        part = pl.ds(row, ROWS)
        values = [
            m[0, part, :] + m[10, part, :],
            m[2, part, :] + m[1, part, :],
            m[4, part, :] + m[3, part, :],
            jnp.where(place < final, m[6, part, :] + m[5, part, :], 0.0),
            jnp.where(place < final - 1, m[8, part, :] + m[7, part, :], 0.0),
        ]
        return [(store_whole, b, q, row, value) for q, value in enumerate(values)]

    sweep(size, rows)
    first_wide(c, b, f, 5, size)
    lowest = jnp.where(place > 0, 0, 1)
    highest = jnp.where(place < final, 2, 1)
    smooth_wide(c, b, f, s, 3, size, lambda q: jnp.logical_and(q >= lowest, q <= highest))
    out = [go.untiled(s.at[1], smooth.at[0])]
    residual_wide(c, b, s, t, 1, size)
    top = thin_rows(t, 0, 0, size // 4)
    bottom = thin_rows(t, 0, half, size // 4)
    result = project(top, mat[0]) + project(bottom, mat[1])
    w[...] = jnp.broadcast_to(result[None], w.shape)
    out.append(go.start(w, copies))
    for copy in out:
        copy.wait()


def coarse_level(scalars, own, sibling, coef, solution, e, o, c, w, p0, p1, g, y, sems):
    core = scalars[0]
    even = core == 0
    half, size, lanes = coef.shape
    go = Copies(sems)
    loads = [
        go.start(coef, c.at[pl.ds(1, half)]),
        go.choose(even, own, sibling, e),
        go.choose(even, sibling, own, o.at[pl.ds(1, 2 * half)]),
    ]
    o[0] = jnp.zeros(o.shape[1:], F32)
    loads[0].wait()
    lane = lax.broadcasted_iota(jnp.int32, (size, lanes), 1)
    row = lax.broadcasted_iota(jnp.int32, (size, lanes), 0)
    upper = lane >= size
    low_edge = (lane % size) == 0
    high_edge = (lane % size) == size - 1
    c[0] = jnp.where(upper, pltpu.roll(c[half], size, 1), 0.0)
    c[half + 1] = jnp.where(upper, 0.0, pltpu.roll(c[1], size, 1))

    edges = [row == size - 1, row == 0, high_edge, low_edge]
    for copy in loads[1:]:
        copy.wait()
    short = lax.broadcasted_iota(jnp.int32, (size // 2, lanes), 1) >= size

    def prepare(q, carry):
        here = c[q + 1]
        sides = [
            pltpu.roll(here, size - 1, 0), pltpu.roll(here, 1, 0),
            pltpu.roll(here, lanes - 1, 1), pltpu.roll(here, 1, 1),
        ]
        sides = [jnp.where(edge, 0.0, value) for edge, value in zip(edges, sides)]
        sides += [c[q], c[q + 2]]
        inverse = 1.0 / (3.0 * here + 0.5 * total(sides))
        scaled = 0.5 * inverse
        for d, side in enumerate(sides):
            weight = (here + side) * scaled
            if d < 4:
                weight = jnp.where(edges[d], 0.0, weight)
            elif d == 4:
                weight = jnp.where(jnp.logical_and(q == 0, jnp.logical_not(upper)), 0.0, weight)
            else:
                weight = jnp.where(jnp.logical_and(q == half - 1, upper), 0.0, weight)
            w[d, q] = weight
        lower_rhs = o[q] + 2.0 * e[q] + o[q + 1]
        upper_rhs = o[q + half] + 2.0 * e[q + half] + o[q + half + 1]
        top = jnp.where(short, pltpu.roll(upper_rhs, size, 1), lower_rhs)
        bottom = jnp.where(short, upper_rhs, pltpu.roll(lower_rhs, size, 1))
        scaled_rhs = jnp.concatenate([top, bottom], axis=0) * inverse
        g[q] = scaled_rhs
        p1[q + 1, PAD : PAD + size] = scaled_rhs * (1.0 / CENTER_VALUE)
        p0[q + 1, PAD : PAD + size] = jnp.zeros((size, lanes), F32)
        return carry

    zeros = jnp.zeros((half + 2, PAD, lanes), F32)
    for p in (p0, p1):
        p[:, :PAD] = zeros
        p[:, PAD + size :] = zeros
    lax.fori_loop(0, half, prepare, 0, unroll=4)
    sigma = CENTER_VALUE / HALF_WIDTH
    rho = 1.0 / sigma
    block = pl.ds(PAD, size)
    for index in range(CHEB - 1):
        older, now = (p0, p1) if index % 2 == 0 else (p1, p0)
        now[0, block] = pltpu.roll(now[half, block], size, 1)
        now[half + 1, block] = pltpu.roll(now[1, block], size, 1)
        rho_new = 1.0 / (2.0 * sigma - rho)
        keep = rho_new * rho
        gain = 2.0 * rho_new / HALF_WIDTH
        rho = rho_new
        final = index == CHEB - 2

        def advance(q, carry):
            values = []
            for start in range(0, size, ROWS):
                part = pl.ds(PAD + start, ROWS)
                flat = pl.ds(start, ROWS)
                here = now[q + 1, part]
                sides = [
                    now[q + 1, pl.ds(PAD + start + 1, ROWS)],
                    now[q + 1, pl.ds(PAD + start - 1, ROWS)],
                    pltpu.roll(here, lanes - 1, 1), pltpu.roll(here, 1, 1),
                    now[q, part], now[q + 2, part],
                ]
                near = total([w[d, q, flat] * side for d, side in enumerate(sides)])
                remains = (g[q, flat] - here) + near
                values.append(here + keep * (here - older[q + 1, part]) + gain * remains)
            for index, value in enumerate(values):
                start = index * ROWS
                if final:
                    flat = pl.ds(start, ROWS)
                    y[q, flat] = value[:, :size]
                    y[q + half, flat] = pltpu.roll(value, size, 1)[:, :size]
                else:
                    older[q + 1, pl.ds(PAD + start, ROWS)] = value
            return carry

        lax.fori_loop(0, half, advance, 0, unroll=UNROLL)
    copy = go.start(y, solution)
    copy.wait()


def vm(*dims):
    return pltpu.VMEM(dims, F32)


def tiled(planes, size):
    return vm(planes, size // LANES, size + 2 * PAD, LANES)


def swapped(value, pairs):
    return lax.ppermute(value, "box", pairs)


def local(rhs_fine, coef_zero, coef_one, coef_two, coef_three):
    count = lax.axis_size("box")
    place = lax.axis_index("box")
    core = place % 2
    scalars = jnp.stack([core, place, jnp.int32(count - 1)]).astype(jnp.int32)
    near = [(i, i ^ 1) for i in range(count)]
    far = [(i, i + 1) for i in range(1, count - 1, 2)]
    far = far + [(j, i) for i, j in far]

    def onward(value, distance):
        route = [(i, i + distance) for i in range(count) if 0 <= i + distance < count]
        return lax.ppermute(value, "box", route)

    n = coef_zero.shape[1]
    n1, n2 = n // 2, n // 4
    n3 = n // 8
    plane = n * n * 4
    matrix0 = jnp.asarray(restriction_matrix(n, n1, 0), BF16)
    matrix1 = jnp.asarray(restriction_matrix(n1, n2, 0), BF16)
    both = np.stack([restriction_matrix(n2, 2 * n3, 0), restriction_matrix(n2, 2 * n3, n3)])
    matrix2 = jnp.asarray(both, BF16)

    def side_plane(field, where):
        return lax.dynamic_index_in_dim(field, where, 0, keepdims=False)

    coef_outer = swapped(side_plane(coef_zero, 3 * core), far)
    coef_sibling = swapped(side_plane(coef_zero, 3 - 3 * core), near)
    first, partial = call(
        first_inner, [shape(2, n, n), shape(2, n, n)],
        [tiled(4, n), vm(2, n, n), vm(2, n, n), vm(2, n, n)], 24, 40 * n * n, 12 * plane, 32,
    )(scalars, coef_zero, rhs_fine)
    first_outer, first_sibling = call(
        first_rim, [shape(n, n), shape(n, n)],
        [vm(2, n, n)] * 4, 8, 10 * n * n, 8 * plane, 32,
    )(scalars, rhs_fine, partial, coef_outer, coef_sibling)

    halo_outer = swapped(first_outer, far)
    halo_sibling = swapped(first_sibling, near)
    smooth, known, factor = call(
        smooth_inner, [shape(4, n, n), shape(2, n, n), shape(2, n, n)],
        [tiled(6, n), tiled(6, n), vm(4, n, n), vm(2, n, n), vm(2, n, n), vm(2, n, n)],
        54, 160 * n * n, 20 * plane, 32,
    )(scalars, coef_zero, rhs_fine, coef_outer, coef_sibling, first, first_outer, first_sibling)
    def folded(field):
        return jnp.concatenate([field[: n2 // 2], field[n2 // 2 :]], axis=1)

    own_two = folded(coef_two[0])
    coefs = jnp.concatenate([coef_one[0], coef_one[1], own_two], axis=0)
    coefs_sibling = swapped(coefs, near)
    coefs_outer = swapped(coefs, far)
    known, coefs_sibling, coefs_outer = lax.optimization_barrier(
        (known, coefs_sibling, coefs_outer)
    )
    smooth_zero, smooth_outer, smooth_sibling = call(
        smooth_rim, [shape(4, n, n), shape(n, n), shape(n, n)],
        [vm(2, n, n)] * 4, 10, 4 * n * n, 10 * plane, 32, {1: 0},
    )(scalars, smooth, known, factor, halo_outer, halo_sibling)

    halo_outer = swapped(smooth_outer, far)
    halo_sibling = swapped(smooth_sibling, near)

    lowered, known, factor = call(
        residual_inner, [shape(2, n1, n1), shape(2, n, n), shape(2, n, n)],
        [tiled(6, n), tiled(6, n), vm(4, n, n), vm(2, n, n), vm(2, n, n),
         tiled(2, n), vm(2, n1, n1), pltpu.VMEM((n, n1), BF16)],
        54, 160 * n * n, 20 * plane, 32,
    )(scalars, coef_zero, rhs_fine, coef_outer, coef_sibling, smooth_zero, smooth_outer,
      smooth_sibling, matrix0)
    left_two = jnp.where(core == 0, coefs_outer[2 * n1 :], coefs_sibling[2 * n1 :])
    right_two = jnp.where(core == 0, coefs_sibling[2 * n1 :], coefs_outer[2 * n1 :])
    coefs_before = onward(jnp.concatenate([coef_one[1], own_two, left_two], axis=0), 2)
    coefs_after = onward(jnp.concatenate([coef_one[0], own_two, right_two], axis=0), -2)
    lowered, coefs_before, coefs_after = lax.optimization_barrier(
        (lowered, coefs_before, coefs_after)
    )
    (packed,) = call(
        residual_rim, [shape(3, n1, n1)],
        [vm(2, n, n), vm(2, n, n), vm(2, n, n), tiled(2, n), vm(4, n1, n1), vm(3, n1, n1),
         pltpu.VMEM((n, n1), BF16)],
        10, 20 * n * n, 8 * plane, 32,
    )(scalars, known, factor, halo_outer, halo_sibling, lowered, matrix0)

    packed_outer = swapped(packed, far)
    packed_before = onward(packed[2], 2)
    packed_sibling = swapped(packed, near)
    smooth_one, packed = call(
        middle_level, [shape(2, n1, n1), shape(2, n2, n2)],
        [vm(10, n1, n1), vm(6, n1, n1), tiled(8, n1), tiled(6, n1),
         tiled(4, n1), tiled(2, n1), vm(2, n2, n2), pltpu.VMEM((n1, n2), BF16)],
        40, 400 * n1 * n1, 24 * n1 * n1 * 4, 40,
    )(scalars, packed, packed_sibling, packed_outer, packed_before, coef_one, coefs_sibling,
      coefs_outer, coefs_before, coefs_after, matrix1)

    packed_outer = swapped(packed, far)
    packed_before = onward(packed, 2)
    packed_after = onward(packed, -2)
    packed_rim = onward(packed[1], 3)
    packed_sibling = swapped(packed, near)
    groups = [[i for i in range(count) if i % 2 == r] for r in range(2)]
    smooth_two, copies = call(
        last_level, [shape(1, n2, n2), shape(count // 2, n3 // 2, 2 * n3)],
        [vm(11, n2, n2), vm(5, n2, n2), tiled(7, n2), tiled(5, n2),
         tiled(3, n2), tiled(1, n2), vm(count // 2, n3 // 2, 2 * n3),
         pltpu.VMEM((2, n2, 2 * n3), BF16)],
        24, 300 * n2 * n2, 40 * n2 * n2 * 4, 40,
    )(scalars, packed, packed_sibling, packed_outer, packed_before, packed_after, packed_rim,
      coef_two, coefs_sibling, coefs_outer, coefs_before, coefs_after, matrix2)

    gathered = lax.all_to_all(copies, "box", 0, 0, tiled=True, axis_index_groups=groups)
    gathered_sibling = swapped(gathered, near)
    half = n3 // 2
    coef_pair = jnp.concatenate([coef_three[:half], coef_three[half:]], axis=2)
    (coarse_solution,) = call(
        coarse_level, [shape(n3, n3, n3)],
        [vm(n3, half, 2 * n3), vm(n3 + 1, half, 2 * n3), vm(half + 2, n3, 2 * n3),
         vm(6, half, n3, 2 * n3), vm(half + 2, n3 + 16, 2 * n3), vm(half + 2, n3 + 16, 2 * n3), vm(half, n3, 2 * n3),
         vm(n3, n3, n3)],
        4, 300 * n3 * n3 * n3, 20 * n3 * n3 * n3, 48,
    )(scalars, gathered, gathered_sibling, coef_pair)
    return (smooth_zero, smooth_one, smooth_two, coarse_solution)


def solution(mesh):
    placed = (
        P("box", None, None),
        P("box", None, None),
        P("box", None, None),
        P("box", None, None),
        P(),
    )
    return jax.shard_map(
        local,
        mesh=mesh,
        in_specs=placed,
        out_specs=(P("box", None, None), P("box", None, None), P("box", None, None), P()),
        check_vma=False,
    )
```

```python
import jax
import jax.numpy as jnp
import numpy as np
from jax import lax
from jax.experimental import pallas as pl
from jax.experimental.pallas import tpu as pltpu
from jax.sharding import PartitionSpec as P

CHEB = 16
OMEGA = 0.8
CENTER_VALUE = 1.04
HALF_WIDTH = 0.96
ROWS = 8
UNROLL = 16
PAD = 8
LANES = 128
F32 = jnp.float32
BF16 = jnp.bfloat16


def restriction_matrix(fine, coarse_lanes, shift):
    weights = np.zeros((fine, coarse_lanes), np.float32)
    for k in range(fine // 2):
        weights[2 * k, k + shift] = 0.5
        weights[2 * k + 1, k + shift] = 0.25
        if k > 0:
            weights[2 * k - 1, k + shift] = 0.25
    return weights


def shape(*dims):
    return jax.ShapeDtypeStruct(dims, F32)


def call(body, outs, scratch, copies, flops, moved, megabytes, aliases=None):
    sems = [pltpu.SemaphoreType.DMA((copies,))]

    def run(scalars, *arrays):
        return pl.pallas_call(
            body,
            out_shape=outs,
            in_specs=[pl.BlockSpec(memory_space=pltpu.SMEM)]
            + [pl.BlockSpec(memory_space=pl.ANY)] * len(arrays),
            out_specs=[pl.BlockSpec(memory_space=pl.ANY)] * len(outs),
            scratch_shapes=scratch + sems,
            input_output_aliases=aliases or {},
            compiler_params=pltpu.CompilerParams(vmem_limit_bytes=megabytes << 20),
            cost_estimate=pl.CostEstimate(flops=flops, bytes_accessed=moved, transcendentals=0),
        )(scalars, *arrays)

    return run


class Group:
    def __init__(self, copies):
        self.copies = list(copies)

    def wait(self):
        for copy in self.copies:
            copy.wait()


class Copies:
    def __init__(self, sems):
        self.sems = sems
        self.used = 0

    def start(self, source, target):
        copy = pltpu.make_async_copy(source, target, self.sems.at[self.used])
        self.used += 1
        copy.start()
        return copy

    def tiles(self, source, target, rows=None):
        rows = source.shape[0] if rows is None else rows
        return Group(
            self.start(source.at[:, columns(t)], target.at[t, pl.ds(PAD, rows), :])
            for t in range(source.shape[1] // LANES)
        )

    def untiled(self, source, target):
        rows = target.shape[0]
        return Group(
            self.start(source.at[t, pl.ds(PAD, rows), :], target.at[:, columns(t)])
            for t in range(target.shape[1] // LANES)
        )

    def choose(self, first_if, source, other, target):
        copy = pltpu.make_async_copy(source, target, self.sems.at[self.used])
        swap = pltpu.make_async_copy(other, target, self.sems.at[self.used])
        self.used += 1

        @pl.when(first_if)
        def _():
            copy.start()

        @pl.when(jnp.logical_not(first_if))
        def _():
            swap.start()

        return copy


def clear_pads(tiles, size):
    zeros = jnp.zeros(tiles.shape[:2] + (PAD, LANES), F32)
    tiles[:, :, :PAD, :] = zeros
    tiles[:, :, PAD + size :, :] = zeros


def clear_top(tiles):
    tiles[:, :, :PAD, :] = jnp.zeros(tiles.shape[:2] + (PAD, LANES), F32)


def columns(tile):
    return pl.ds(tile * LANES, LANES)


def load_rows(ref, plane, row, offset=0):
    return [ref[plane, t, pl.ds(PAD + row + offset, ROWS), :] for t in range(ref.shape[1])]


def load_flat(ref, plane, row):
    part = pl.ds(row, ROWS)
    return [ref[plane, part, columns(t)] for t in range(ref.shape[2] // LANES)]


def store_rows(ref, plane, row, values):
    for t, value in enumerate(values):
        ref[plane, t, pl.ds(PAD + row, ROWS), :] = value


def store_flat(ref, plane, row, values):
    for t, value in enumerate(values):
        ref[plane, pl.ds(row, ROWS), columns(t)] = value


def store_whole(ref, plane, row, value):
    ref[plane, pl.ds(row, ROWS), :] = value


def each(function, *lists):
    return [function(*values) for values in zip(*lists)]


def lane_sides(centre):
    lane = lax.broadcasted_iota(jnp.int32, (ROWS, LANES), 1)
    first = lane == 0
    last = lane == LANES - 1
    up = [pltpu.roll(value, 1, 1) for value in centre]
    down = [pltpu.roll(value, LANES - 1, 1) for value in centre]
    left = [jnp.where(first, up[t - 1] if t else 0.0, up[t]) for t in range(len(centre))]
    right = [
        jnp.where(last, down[t + 1] if t + 1 < len(centre) else 0.0, down[t])
        for t in range(len(centre))
    ]
    return [left, right]


def around(ref, plane, row, sides):
    centre = load_rows(ref, plane, row)
    beside = lane_sides(centre)
    beside += [load_rows(ref, plane, row, 1), load_rows(ref, plane, row, -1)]
    beside += [load_rows(ref, plane + side, row) for side in sides]
    return centre, beside


def face_totals(coef, beside):
    result = each(lambda c, s: c + s, coef, beside[0])
    for side in beside[1:]:
        result = each(lambda r, c, s: r + (c + s), result, coef, side)
    return result


def stencil(coefs, fields, row, coef_plane, field_plane, sides):
    coef, coef_beside = around(coefs, coef_plane, row, sides)
    here, beside = around(fields, field_plane, row, sides)
    weights = [each(lambda c, s: c + s, coef, side) for side in coef_beside]
    twice = weights[0]
    gathered = each(lambda w, v: w * v, weights[0], beside[0])
    for weight, side in zip(weights[1:], beside[1:]):
        twice = each(lambda a, b: a + b, twice, weight)
        gathered = each(lambda a, w, v: a + w * v, gathered, weight, side)
    return twice, gathered, here, coef


def first_of(rhs, twice):
    return each(lambda b, d: (2.0 * OMEGA) * b / d, rhs, twice)


def smoothed_of(rhs, twice, gathered, here):
    return each(
        lambda b, d, g, v: (1.0 - OMEGA) * v + ((2.0 * OMEGA) * b + OMEGA * g) / d,
        rhs, twice, gathered, here,
    )


def residual_of(rhs, twice, gathered, here):
    return each(lambda b, d, g, v: b - 0.5 * (d * v - g), rhs, twice, gathered, here)


def total(values):
    result = values[0]
    for value in values[1:]:
        result = result + value
    return result


def sweep(size, body, start=0):
    def step(index, carry):
        for store, ref, plane, row, values in body(pl.multiple_of(index * ROWS, ROWS)):
            store(ref, plane, row, values)
        return carry

    lax.fori_loop(start // ROWS, size // ROWS, step, 0, unroll=UNROLL)


def in_halves(size):
    return ((0, size // 2), (size // 2, size))


def thin_rows(tiles, plane, start, count):
    parts = []
    for tile in range(tiles.shape[1]):
        parts.append(
            0.25 * tiles[plane, tile, pl.ds(PAD - 1 + start, count, stride=2), :]
            + 0.5 * tiles[plane, tile, pl.ds(PAD + start, count, stride=2), :]
            + 0.25 * tiles[plane, tile, pl.ds(PAD + 1 + start, count, stride=2), :]
        )
    return jnp.concatenate(parts, axis=1)


def restrict_plane(tiles, plane, size, matrix):
    return project(thin_rows(tiles, plane, 0, size // 2), matrix)


def project(rows, matrix):
    high = rows.astype(BF16)
    rest = rows - high.astype(F32)
    middle = rest.astype(BF16)
    low = (rest - middle.astype(F32)).astype(BF16)
    return (
        jnp.dot(low, matrix, preferred_element_type=F32)
        + jnp.dot(middle, matrix, preferred_element_type=F32)
        + jnp.dot(high, matrix, preferred_element_type=F32)
    )


def plane_at(core, place):
    return place + core * (3 - 2 * place)


def first_inner(scalars, coef, rhs, first, partial, c, b, f, g, sems):
    core = scalars[0]
    size = coef.shape[1]
    go = Copies(sems)
    waits = [go.tiles(coef.at[plane_at(core, q)], c.at[q]) for q in (0, 1)]
    later = [[go.tiles(coef.at[plane_at(core, 2)], c.at[2])]]
    later[0].append(go.start(rhs.at[plane_at(core, 1)], b.at[0]))
    later.append([go.tiles(coef.at[plane_at(core, 3)], c.at[3])])
    later[1].append(go.start(rhs.at[plane_at(core, 2)], b.at[1]))
    clear_pads(c, size)
    for copy in waits:
        copy.wait()
    out = []

    def partial_plane(slot, q, side):
        def rows(row):
            coef_here, beside = around(c, q, row, (side,))
            twice = face_totals(coef_here, beside)
            return [(store_flat, g, slot, row, each(lambda d, v: d + v, twice, coef_here))]

        sweep(size, rows)
        out.append(go.start(g.at[slot], partial.at[slot]))

    def first_plane(q):
        def rows(row):
            twice = face_totals(*around(c, q, row, (-1, 1)))
            return [(store_flat, f, q - 1, row, first_of(load_flat(b, q - 1, row), twice))]

        sweep(size, rows)
        out.append(go.start(f.at[q - 1], first.at[q - 1]))

    partial_plane(0, 0, 1)
    for copy in later[0]:
        copy.wait()
    first_plane(1)
    for copy in later[1]:
        copy.wait()
    first_plane(2)
    partial_plane(1, 3, -1)
    for copy in out:
        copy.wait()


def first_rim(scalars, rhs, partial, coef_outer, coef_sibling, outer, sibling, b, g, h, f, sems):
    core = scalars[0]
    size = rhs.shape[1]
    go = Copies(sems)
    loads = []
    for slot, q, halo in ((1, 3, coef_sibling), (0, 0, coef_outer)):
        for start, stop in in_halves(size):
            part = pl.ds(start, stop - start)
            loads.append(
                [
                    go.start(rhs.at[plane_at(core, q), part], b.at[slot, part]),
                    go.start(partial.at[slot, part], g.at[slot, part]),
                    go.start(halo.at[part], h.at[slot, part]),
                ]
            )
    out = []
    for slot, target in ((1, sibling), (0, outer)):
        for start, stop in in_halves(size):
            for copy in loads.pop(0):
                copy.wait()

            def rows(row):
                twice = each(lambda g, h: g + h, load_flat(g, slot, row), load_flat(h, slot, row))
                return [(store_flat, f, slot, row, first_of(load_flat(b, slot, row), twice))]

            sweep(stop, rows, start)
            part = pl.ds(start, stop - start)
            out.append(go.start(f.at[slot, part], target.at[part]))
    for copy in out:
        copy.wait()


def loads_in_order(go, core, coef, rhs, coef_outer, coef_sibling, sources, c, v, b):
    def coef_in(q):
        if q == 0:
            return go.tiles(coef_outer, c.at[0])
        if q == 5:
            return go.tiles(coef_sibling, c.at[5])
        return go.tiles(coef.at[plane_at(core, q - 1)], c.at[q])

    def field_in(q):
        return go.tiles(sources[q - 1], v.at[q])

    def rhs_in(q):
        return go.start(rhs.at[plane_at(core, q - 1)], b.at[q - 1])

    waits = [[coef_in(0), coef_in(1), coef_in(2), field_in(1), field_in(2), rhs_in(1)]]
    waits.append([coef_in(3), field_in(3), rhs_in(2)])
    waits.append([coef_in(4), field_in(4), rhs_in(3)])
    waits.append([coef_in(5), rhs_in(4)])
    return waits


def smooth_inner(
    scalars, coef, rhs, coef_outer, coef_sibling, first, first_outer, first_sibling,
    smooth, known, factor, c, v, b, s, g, h, sems,
):
    core = scalars[0]
    size = coef.shape[1]
    go = Copies(sems)
    sources = (first_outer, first.at[0], first.at[1], first_sibling)
    waits = loads_in_order(go, core, coef, rhs, coef_outer, coef_sibling, sources, c, v, b)
    clear_pads(c, size)
    clear_pads(v, size)
    out = []

    def rim(slot, q, side):
        def rows(row):
            twice, gathered, here, coef_here = stencil(c, v, row, q, q, (side,))
            edge = each(lambda c, h: c + h, coef_here, load_rows(c, q - side, row))
            twice = each(lambda d, e: d + e, twice, edge)
            scale = [1.0 / value for value in twice]
            known_rows = each(
                lambda b, d, g, v: (1.0 - OMEGA) * v + ((2.0 * OMEGA) * b + OMEGA * g) * d,
                load_flat(b, q - 1, row), scale, gathered, here,
            )
            factor_rows = each(lambda d, e: (OMEGA * e) * d, scale, edge)
            return [(store_flat, g, slot, row, known_rows), (store_flat, h, slot, row, factor_rows)]

        sweep(size, rows)
        out.append(go.start(g.at[slot], known.at[slot]))
        out.append(go.start(h.at[slot], factor.at[slot]))

    def middle(q):
        def rows(row):
            twice, gathered, here, _ = stencil(c, v, row, q, q, (-1, 1))
            values = smoothed_of(load_flat(b, q - 1, row), twice, gathered, here)
            return [(store_flat, s, q - 2, row, values)]

        sweep(size, rows)
        out.append(go.start(s.at[q - 2], smooth.at[plane_at(core, q - 1)]))

    steps = ((rim, (0, 1, 1)), (middle, (2,)), (middle, (3,)), (rim, (1, 4, -1)))
    for needed, (work, arguments) in zip(waits, steps):
        for copy in needed:
            copy.wait()
        work(*arguments)
    for copy in out:
        copy.wait()


def rim_loads(go, known, factor, halo_outer, halo_sibling, g, h, v):
    loads = []
    for slot, halo in ((1, halo_sibling), (0, halo_outer)):
        for start, stop in in_halves(known.shape[1]):
            part = pl.ds(start, stop - start)
            loads.append(
                [
                    go.start(known.at[slot, part], g.at[slot, part]),
                    go.start(factor.at[slot, part], h.at[slot, part]),
                    go.start(halo.at[part], v.at[slot, part]),
                ]
            )
    return loads


def smooth_rim(
    scalars, started, known, factor, halo_outer, halo_sibling,
    smooth, outer, sibling, g, h, v, s, sems,
):
    core = scalars[0]
    size = known.shape[1]
    go = Copies(sems)
    loads = rim_loads(go, known, factor, halo_outer, halo_sibling, g, h, v)
    out = []
    for slot, q, target in ((1, 3, sibling), (0, 0, outer)):
        for start, stop in in_halves(size):
            for copy in loads.pop(0):
                copy.wait()

            def rows(row):
                flat = [load_flat(ref, slot, row) for ref in (g, h, v)]
                return [(store_flat, s, slot, row, each(lambda g, h, v: g + h * v, *flat))]

            sweep(stop, rows, start)
            part = pl.ds(start, stop - start)
            out.append(go.start(s.at[slot, part], target.at[part]))
            out.append(go.start(s.at[slot, part], smooth.at[plane_at(core, q), part]))
    for copy in out:
        copy.wait()


def residual_inner(
    scalars, coef, rhs, coef_outer, coef_sibling, smooth, smooth_outer, smooth_sibling, matrix,
    lowered, known, factor, c, v, b, g, h, t, low, mat, sems,
):
    core = scalars[0]
    size = coef.shape[1]
    go = Copies(sems)
    sources = (
        smooth_outer, smooth.at[plane_at(core, 1)], smooth.at[plane_at(core, 2)], smooth_sibling,
    )
    waits = loads_in_order(go, core, coef, rhs, coef_outer, coef_sibling, sources, c, v, b)
    waits[0].append(go.start(matrix, mat))
    clear_pads(c, size)
    clear_pads(v, size)
    clear_top(t)
    out = []

    def rim(slot, q, side):
        def rows(row):
            twice, gathered, here, coef_here = stencil(c, v, row, q, q, (side,))
            edge = each(lambda c, h: c + h, coef_here, load_rows(c, q - side, row))
            twice = each(lambda d, e: d + e, twice, edge)
            known_rows = residual_of(load_flat(b, q - 1, row), twice, gathered, here)
            factor_rows = [0.5 * value for value in edge]
            return [(store_flat, g, slot, row, known_rows), (store_flat, h, slot, row, factor_rows)]

        sweep(size, rows)
        out.append(go.start(g.at[slot], known.at[slot]))
        out.append(go.start(h.at[slot], factor.at[slot]))

    def middle(q):
        def rows(row):
            twice, gathered, here, _ = stencil(c, v, row, q, q, (-1, 1))
            values = residual_of(load_flat(b, q - 1, row), twice, gathered, here)
            return [(store_rows, t, q - 2, row, values)]

        sweep(size, rows)
        low[q - 2] = restrict_plane(t, q - 2, size, mat[...])

    steps = ((rim, (0, 1, 1)), (middle, (2,)), (middle, (3,)), (rim, (1, 4, -1)))
    for needed, (work, arguments) in zip(waits, steps):
        for copy in needed:
            copy.wait()
        work(*arguments)
    out.append(go.start(low, lowered))
    for copy in out:
        copy.wait()


def residual_rim(
    scalars, known, factor, halo_outer, halo_sibling, lowered, matrix,
    packed, g, h, v, t, low, pack, mat, sems,
):
    core = scalars[0]
    size = known.shape[1]
    go = Copies(sems)
    more = [go.start(lowered, low.at[pl.ds(1, 2)]), go.start(matrix, mat)]
    loads = rim_loads(go, known, factor, halo_outer, halo_sibling, g, h, v)
    clear_top(t)
    for copy in more:
        copy.wait()
    for slot in (1, 0):
        for start, stop in in_halves(size):
            for copy in loads.pop(0):
                copy.wait()

            def rows(row):
                flat = [load_flat(ref, slot, row) for ref in (g, h, v)]
                return [(store_rows, t, slot, row, each(lambda g, h, v: g + h * v, *flat))]

            sweep(stop, rows, start)
        low[3 * slot] = restrict_plane(t, slot, size, mat[...])
    one = plane_at(core, 1)
    two = plane_at(core, 2)
    last = low[plane_at(core, 3)]
    pack[0] = 2.0 * low[plane_at(core, 0)] + low[one]
    pack[1] = low[one] + 2.0 * low[two] + last
    pack[2] = last
    copy = go.start(pack, packed)
    copy.wait()


def guarded(values):
    return [jnp.where(value == 0.0, 1.0, value) for value in values]


def first_wide(c, b, f, planes, size):
    def plane(q):
        def rows(row):
            twice = guarded(face_totals(*around(c, q + 1, row, (-1, 1))))
            return [(store_rows, f, q, row, first_of(load_flat(b, q, row), twice))]

        sweep(size, rows)

    pl.loop(0, planes)(plane)


def smooth_wide(c, b, f, s, planes, size, inside):
    def plane(q):
        keep = inside(q)

        def rows(row):
            twice, gathered, here, _ = stencil(c, f, row, q + 2, q + 1, (-1, 1))
            values = smoothed_of(load_flat(b, q + 1, row), guarded(twice), gathered, here)
            return [(store_rows, s, q, row, [jnp.where(keep, value, 0.0) for value in values])]

        sweep(size, rows)

    pl.loop(0, planes)(plane)


def residual_wide(c, b, s, t, planes, size):
    for q in range(planes):

        def rows(row):
            twice, gathered, here, _ = stencil(c, s, row, q + 3, q + 1, (-1, 1))
            values = residual_of(load_flat(b, q + 2, row), twice, gathered, here)
            return [(store_rows, t, q, row, values)]

        sweep(size, rows)


def middle_level(
    scalars, own, sibling, outer, rim_outer, rim_sibling, coef, coef_sibling, coef_outer,
    coef_beyond, matrix, smooth, packed, m, b, c, f, s, t, pack, mat, sems,
):
    core = scalars[0]
    place = scalars[1]
    final = scalars[2]
    size = coef.shape[1]
    even = core == 0
    go = Copies(sems)
    three = pl.ds(0, 3)
    loads = [
        go.start(own, m.at[pl.ds(3, 3)]),
        go.choose(even, outer, sibling, m.at[three]),
        go.choose(even, sibling, outer, m.at[pl.ds(6, 3)]),
        go.choose(even, rim_outer, rim_sibling, m.at[9]),
        go.start(matrix, mat),
    ]
    for tile in range(size // LANES):
        part = columns(tile)
        for q in range(2):
            left = c.at[1 + q, tile, pl.ds(PAD, size), :]
            right = c.at[5 + q, tile, pl.ds(PAD, size), :]
            loads.append(go.choose(even, coef_outer.at[q, :, part], coef_sibling.at[q, :, part], left))
            loads.append(go.choose(even, coef_sibling.at[q, :, part], coef_outer.at[q, :, part], right))
        left = c.at[0, tile, pl.ds(PAD, size), :]
        right = c.at[7, tile, pl.ds(PAD, size), :]
        loads.append(go.choose(even, coef_outer.at[2, :, part], coef_beyond.at[:, part], left))
        loads.append(go.choose(even, coef_beyond.at[:, part], coef_outer.at[2, :, part], right))
    loads += [go.tiles(coef.at[q], c.at[3 + q]) for q in range(2)]
    clear_pads(c, size)
    clear_pads(f, size)
    clear_pads(s, size)
    clear_top(t)
    for copy in loads:
        copy.wait()

    def rows(row):
        part = pl.ds(row, ROWS)
        values = [
            m[0, part, :] + m[9, part, :],
            m[1, part, :],
            m[3, part, :] + m[2, part, :],
            m[4, part, :],
            jnp.where(place < final, m[6, part, :] + m[5, part, :], 0.0),
            m[7, part, :],
        ]
        return [(store_whole, b, q, row, value) for q, value in enumerate(values)]

    sweep(size, rows)
    first_wide(c, b, f, 6, size)
    lowest = jnp.where(place > 0, 0, 1)
    highest = jnp.where(place < final, 3, 2)
    smooth_wide(c, b, f, s, 4, size, lambda q: jnp.logical_and(q >= lowest, q <= highest))
    out = [go.untiled(s.at[1 + q], smooth.at[q]) for q in range(2)]
    residual_wide(c, b, s, t, 2, size)
    low = restrict_plane(t, 1, size, mat[...])
    pack[0] = 2.0 * restrict_plane(t, 0, size, mat[...]) + low
    pack[1] = low
    out.append(go.start(pack, packed))
    for copy in out:
        copy.wait()


def last_level(
    scalars, own, sibling, even_chip, odd_chip, even_beside, odd_beside, third, matrices,
    smooth, copies, n, b, c, f, s, t, w, mat, sems,
):
    core = scalars[0]
    place = scalars[1]
    final = scalars[2]
    size = own.shape[1]
    half = size // 2
    left_core = core == 0
    left_is_odd = (place // 2) % 2 == 0
    go = Copies(sems)
    nearer = [
        go.start(own, n.at[3]),
        go.start(sibling, n.at[jnp.where(left_core, 4, 2)]),
        go.choose(left_is_odd, odd_chip, even_chip, n.at[1]),
        go.choose(left_is_odd, even_chip, odd_chip, n.at[5]),
        go.choose(left_is_odd, odd_beside, even_beside, n.at[jnp.where(left_core, 2, 0)]),
        go.choose(left_is_odd, even_beside, odd_beside, n.at[jnp.where(left_core, 6, 4)]),
        go.start(third, n.at[jnp.where(left_core, 0, 6), pl.ds(1, 2)]),
        go.start(matrices, mat),
    ]
    clear_pads(c, size)
    clear_pads(f, size)
    clear_pads(s, size)
    clear_top(t)
    for copy in nearer:
        copy.wait()

    def coef_rows(row):
        return [(store_rows, c, q, row, [n[q, 2, pl.ds(row, ROWS), :]]) for q in range(7)]

    sweep(size, coef_rows)

    def rows(row):
        part = pl.ds(row, ROWS)
        values = [
            n[1, 0, part, :] + n[0, 1, part, :],
            n[2, 0, part, :] + n[1, 1, part, :],
            n[3, 0, part, :] + n[2, 1, part, :],
            jnp.where(place < final, n[4, 0, part, :] + n[3, 1, part, :], 0.0),
            jnp.where(place < final - 1, n[5, 0, part, :] + n[4, 1, part, :], 0.0),
        ]
        return [(store_whole, b, q, row, value) for q, value in enumerate(values)]

    sweep(size, rows)
    first_wide(c, b, f, 5, size)
    lowest = jnp.where(place > 0, 0, 1)
    highest = jnp.where(place < final, 2, 1)
    smooth_wide(c, b, f, s, 3, size, lambda q: jnp.logical_and(q >= lowest, q <= highest))
    out = [go.untiled(s.at[1], smooth.at[0])]
    residual_wide(c, b, s, t, 1, size)
    top = thin_rows(t, 0, 0, size // 4)
    bottom = thin_rows(t, 0, half, size // 4)
    result = project(top, mat[0]) + project(bottom, mat[1])
    w[...] = jnp.broadcast_to(result[None], w.shape)
    out.append(go.start(w, copies))
    for copy in out:
        copy.wait()


def coarse_level(scalars, own, sibling, coef, solution, e, o, c, w, p0, p1, g, y, sems):
    core = scalars[0]
    even = core == 0
    half, size, lanes = coef.shape
    go = Copies(sems)
    loads = [
        go.start(coef, c.at[pl.ds(1, half)]),
        go.choose(even, own, sibling, e),
        go.choose(even, sibling, own, o.at[pl.ds(1, 2 * half)]),
    ]
    o[0] = jnp.zeros(o.shape[1:], F32)
    loads[0].wait()
    lane = lax.broadcasted_iota(jnp.int32, (size, lanes), 1)
    row = lax.broadcasted_iota(jnp.int32, (size, lanes), 0)
    upper = lane >= size
    low_edge = (lane % size) == 0
    high_edge = (lane % size) == size - 1
    c[0] = jnp.where(upper, pltpu.roll(c[half], size, 1), 0.0)
    c[half + 1] = jnp.where(upper, 0.0, pltpu.roll(c[1], size, 1))

    edges = [row == size - 1, row == 0, high_edge, low_edge]
    for copy in loads[1:]:
        copy.wait()
    short = lax.broadcasted_iota(jnp.int32, (size // 2, lanes), 1) >= size

    def prepare(q, carry):
        here = c[q + 1]
        sides = [
            pltpu.roll(here, size - 1, 0), pltpu.roll(here, 1, 0),
            pltpu.roll(here, lanes - 1, 1), pltpu.roll(here, 1, 1),
        ]
        sides = [jnp.where(edge, 0.0, value) for edge, value in zip(edges, sides)]
        sides += [c[q], c[q + 2]]
        inverse = 1.0 / (3.0 * here + 0.5 * total(sides))
        scaled = 0.5 * inverse
        for d, side in enumerate(sides):
            weight = (here + side) * scaled
            if d < 4:
                weight = jnp.where(edges[d], 0.0, weight)
            elif d == 4:
                weight = jnp.where(jnp.logical_and(q == 0, jnp.logical_not(upper)), 0.0, weight)
            else:
                weight = jnp.where(jnp.logical_and(q == half - 1, upper), 0.0, weight)
            w[d, q] = weight
        lower_rhs = o[q] + 2.0 * e[q] + o[q + 1]
        upper_rhs = o[q + half] + 2.0 * e[q + half] + o[q + half + 1]
        top = jnp.where(short, pltpu.roll(upper_rhs, size, 1), lower_rhs)
        bottom = jnp.where(short, upper_rhs, pltpu.roll(lower_rhs, size, 1))
        scaled_rhs = jnp.concatenate([top, bottom], axis=0) * inverse
        g[q] = scaled_rhs
        p1[q + 1, PAD : PAD + size] = scaled_rhs * (1.0 / CENTER_VALUE)
        p0[q + 1, PAD : PAD + size] = jnp.zeros((size, lanes), F32)
        return carry

    zeros = jnp.zeros((half + 2, PAD, lanes), F32)
    for p in (p0, p1):
        p[:, :PAD] = zeros
        p[:, PAD + size :] = zeros
    lax.fori_loop(0, half, prepare, 0, unroll=4)
    sigma = CENTER_VALUE / HALF_WIDTH
    rho = 1.0 / sigma
    block = pl.ds(PAD, size)
    for index in range(CHEB - 1):
        older, now = (p0, p1) if index % 2 == 0 else (p1, p0)
        now[0, block] = pltpu.roll(now[half, block], size, 1)
        now[half + 1, block] = pltpu.roll(now[1, block], size, 1)
        rho_new = 1.0 / (2.0 * sigma - rho)
        keep = rho_new * rho
        gain = 2.0 * rho_new / HALF_WIDTH
        rho = rho_new
        final = index == CHEB - 2

        def advance(q, carry):
            values = []
            for start in range(0, size, ROWS):
                part = pl.ds(PAD + start, ROWS)
                flat = pl.ds(start, ROWS)
                here = now[q + 1, part]
                sides = [
                    now[q + 1, pl.ds(PAD + start + 1, ROWS)],
                    now[q + 1, pl.ds(PAD + start - 1, ROWS)],
                    pltpu.roll(here, lanes - 1, 1), pltpu.roll(here, 1, 1),
                    now[q, part], now[q + 2, part],
                ]
                near = total([w[d, q, flat] * side for d, side in enumerate(sides)])
                remains = (g[q, flat] - here) + near
                values.append(here + keep * (here - older[q + 1, part]) + gain * remains)
            for index, value in enumerate(values):
                start = index * ROWS
                if final:
                    flat = pl.ds(start, ROWS)
                    y[q, flat] = value[:, :size]
                    y[q + half, flat] = pltpu.roll(value, size, 1)[:, :size]
                else:
                    older[q + 1, pl.ds(PAD + start, ROWS)] = value
            return carry

        lax.fori_loop(0, half, advance, 0, unroll=UNROLL)
    copy = go.start(y, solution)
    copy.wait()


def vm(*dims):
    return pltpu.VMEM(dims, F32)


def tiled(planes, size):
    return vm(planes, size // LANES, size + 2 * PAD, LANES)


def swapped(value, pairs):
    return lax.ppermute(value, "box", pairs)


def local(rhs_fine, coef_zero, coef_one, coef_two, coef_three):
    count = lax.axis_size("box")
    place = lax.axis_index("box")
    core = place % 2
    scalars = jnp.stack([core, place, jnp.int32(count - 1)]).astype(jnp.int32)
    near = [(i, i ^ 1) for i in range(count)]
    far = [(i, i + 1) for i in range(1, count - 1, 2)]
    far = far + [(j, i) for i, j in far]

    n = coef_zero.shape[1]
    n1, n2 = n // 2, n // 4
    n3 = n // 8
    plane = n * n * 4
    matrix0 = jnp.asarray(restriction_matrix(n, n1, 0), BF16)
    matrix1 = jnp.asarray(restriction_matrix(n1, n2, 0), BF16)
    both = np.stack([restriction_matrix(n2, 2 * n3, 0), restriction_matrix(n2, 2 * n3, n3)])
    matrix2 = jnp.asarray(both, BF16)

    def side_plane(field, where):
        return lax.dynamic_index_in_dim(field, where, 0, keepdims=False)

    coef_outer = side_plane(coef_zero, 3 * core)
    rest, coef_outer = lax.optimization_barrier((coef_zero, coef_outer))
    coef_outer = swapped(coef_outer, far)
    coef_sibling = swapped(side_plane(rest, 3 - 3 * core), near)
    first, partial = call(
        first_inner, [shape(2, n, n), shape(2, n, n)],
        [tiled(4, n), vm(2, n, n), vm(2, n, n), vm(2, n, n)], 24, 40 * n * n, 12 * plane, 60,
    )(scalars, coef_zero, rhs_fine)
    coefs_sibling = swapped(coef_one, near)
    beyond = lax.dynamic_slice_in_dim(coefs_sibling, core, 1, 0)
    coefs_out = jnp.concatenate([coef_one, beyond], axis=0)
    partial, coefs_out = lax.optimization_barrier((partial, coefs_out))
    first_outer, first_sibling = call(
        first_rim, [shape(n, n), shape(n, n)],
        [vm(2, n, n)] * 4, 16, 10 * n * n, 8 * plane, 60,
    )(scalars, rhs_fine, partial, coef_outer, coef_sibling)

    halo_outer = swapped(first_outer, far)
    halo_sibling = swapped(first_sibling, near)
    smooth, known, factor = call(
        smooth_inner, [shape(4, n, n), shape(2, n, n), shape(2, n, n)],
        [tiled(6, n), tiled(6, n), vm(4, n, n), vm(2, n, n), vm(2, n, n), vm(2, n, n)],
        54, 160 * n * n, 20 * plane, 60,
    )(scalars, coef_zero, rhs_fine, coef_outer, coef_sibling, first, first_outer, first_sibling)
    coefs_out, known = lax.optimization_barrier((coefs_out, known))
    coefs_outer = swapped(coefs_out, far)
    smooth_zero, smooth_outer, smooth_sibling = call(
        smooth_rim, [shape(4, n, n), shape(n, n), shape(n, n)],
        [vm(2, n, n)] * 4, 20, 4 * n * n, 10 * plane, 60, {1: 0},
    )(scalars, smooth, known, factor, halo_outer, halo_sibling)

    halo_outer = swapped(smooth_outer, far)
    halo_sibling = swapped(smooth_sibling, near)

    smooth_outer, coefs_outer = lax.optimization_barrier((smooth_outer, coefs_outer))
    lowered, known, factor = call(
        residual_inner, [shape(2, n1, n1), shape(2, n, n), shape(2, n, n)],
        [tiled(6, n), tiled(6, n), vm(4, n, n), vm(2, n, n), vm(2, n, n),
         tiled(2, n), vm(2, n1, n1), pltpu.VMEM((n, n1), BF16)],
        54, 160 * n * n, 20 * plane, 60,
    )(scalars, coef_zero, rhs_fine, coef_outer, coef_sibling, smooth_zero, smooth_outer,
      smooth_sibling, matrix0)
    coefs_beyond = swapped(lax.dynamic_index_in_dim(coefs_outer, 1 - core, 0, False), near)
    lowered, coefs_beyond = lax.optimization_barrier((lowered, coefs_beyond))
    (packed,) = call(
        residual_rim, [shape(3, n1, n1)],
        [vm(2, n, n), vm(2, n, n), vm(2, n, n), tiled(2, n), vm(4, n1, n1), vm(3, n1, n1),
         pltpu.VMEM((n, n1), BF16)],
        15, 20 * n * n, 8 * plane, 60,
    )(scalars, known, factor, halo_outer, halo_sibling, lowered, matrix0)

    packed_outer = swapped(packed, far)
    packed_sibling = swapped(packed, near)
    rim_outer = swapped(packed_sibling[2], far)
    rim_sibling = swapped(packed_outer[2], near)
    smooth_one, packed = call(
        middle_level, [shape(2, n1, n1), shape(2, n2, n2)],
        [vm(10, n1, n1), vm(6, n1, n1), tiled(8, n1), tiled(6, n1),
         tiled(4, n1), tiled(2, n1), vm(2, n2, n2), pltpu.VMEM((n1, n2), BF16)],
        40, 400 * n1 * n1, 24 * n1 * n1 * 4, 40,
    )(scalars, packed, packed_sibling, packed_outer, rim_outer, rim_sibling, coef_one,
      coefs_sibling, coefs_outer, coefs_beyond, matrix1)

    chip_even = [(i, i ^ 2) for i in range(count)]
    chip_odd = [(i, i + 2) for i in range(count - 2) if i & 2]
    chip_odd = chip_odd + [(j, i) for i, j in chip_odd]
    third = [(i, i + 3) for i in range(1, count - 3, 2)]
    third = third + [(j, i) for i, j in third]
    sent = jnp.concatenate([packed, coef_two], axis=0)
    even_chip = swapped(sent, chip_even)
    odd_chip = swapped(sent, chip_odd)
    packed_third = swapped(sent[1:], third)
    packed_sibling = swapped(sent, near)
    even_chip, odd_chip, packed_third = lax.optimization_barrier(
        (even_chip, odd_chip, packed_third)
    )
    even_beside = swapped(even_chip, near)
    odd_beside = swapped(odd_chip, near)
    groups = [[i for i in range(count) if i % 2 == r] for r in range(2)]
    smooth_two, copies = call(
        last_level, [shape(1, n2, n2), shape(count // 2, n3 // 2, 2 * n3)],
        [vm(7, 3, n2, n2), vm(5, n2, n2), tiled(7, n2), tiled(5, n2),
         tiled(3, n2), tiled(1, n2), vm(count // 2, n3 // 2, 2 * n3),
         pltpu.VMEM((2, n2, 2 * n3), BF16)],
        24, 300 * n2 * n2, 40 * n2 * n2 * 4, 40,
    )(scalars, sent, packed_sibling, even_chip, odd_chip, even_beside, odd_beside, packed_third,
      matrix2)

    gathered = lax.all_to_all(copies, "box", 0, 0, tiled=True, axis_index_groups=groups)
    gathered_sibling = swapped(gathered, near)
    half = n3 // 2
    coef_pair = jnp.concatenate([coef_three[:half], coef_three[half:]], axis=2)
    (coarse_solution,) = call(
        coarse_level, [shape(n3, n3, n3)],
        [vm(n3, half, 2 * n3), vm(n3 + 1, half, 2 * n3), vm(half + 2, n3, 2 * n3),
         vm(6, half, n3, 2 * n3), vm(half + 2, n3 + 16, 2 * n3), vm(half + 2, n3 + 16, 2 * n3), vm(half, n3, 2 * n3),
         vm(n3, n3, n3)],
        4, 300 * n3 * n3 * n3, 20 * n3 * n3 * n3, 48,
    )(scalars, gathered, gathered_sibling, coef_pair)
    return (smooth_zero, smooth_one, smooth_two, coarse_solution)


def solution(mesh):
    placed = (
        P("box", None, None),
        P("box", None, None),
        P("box", None, None),
        P("box", None, None),
        P(),
    )
    return jax.shard_map(
        local,
        mesh=mesh,
        in_specs=placed,
        out_specs=(P("box", None, None), P("box", None, None), P("box", None, None), P()),
        check_vma=False,
    )
```

```python
import jax
import jax.numpy as jnp
import numpy as np
from jax import lax
from jax.experimental import pallas as pl
from jax.experimental.pallas import tpu as pltpu
from jax.sharding import PartitionSpec as P

CHEB = 16
OMEGA = 0.8
CENTER_VALUE = 1.04
HALF_WIDTH = 0.96
ROWS = 8
UNROLL = 16
PAD = 8
LANES = 128
F32 = jnp.float32
BF16 = jnp.bfloat16


def restriction_matrix(fine, coarse_lanes, shift):
    weights = np.zeros((fine, coarse_lanes), np.float32)
    for k in range(fine // 2):
        weights[2 * k, k + shift] = 0.5
        weights[2 * k + 1, k + shift] = 0.25
        if k > 0:
            weights[2 * k - 1, k + shift] = 0.25
    return weights


def shape(*dims):
    return jax.ShapeDtypeStruct(dims, F32)


def call(body, outs, scratch, copies, flops, moved, megabytes, aliases=None):
    sems = [pltpu.SemaphoreType.DMA((copies,))]

    def run(scalars, *arrays):
        return pl.pallas_call(
            body,
            out_shape=outs,
            in_specs=[pl.BlockSpec(memory_space=pltpu.SMEM)]
            + [pl.BlockSpec(memory_space=pl.ANY)] * len(arrays),
            out_specs=[pl.BlockSpec(memory_space=pl.ANY)] * len(outs),
            scratch_shapes=scratch + sems,
            input_output_aliases=aliases or {},
            compiler_params=pltpu.CompilerParams(vmem_limit_bytes=megabytes << 20),
            cost_estimate=pl.CostEstimate(flops=flops, bytes_accessed=moved, transcendentals=0),
        )(scalars, *arrays)

    return run


class Group:
    def __init__(self, copies):
        self.copies = list(copies)

    def wait(self):
        for copy in self.copies:
            copy.wait()


class Copies:
    def __init__(self, sems):
        self.sems = sems
        self.used = 0

    def start(self, source, target):
        copy = pltpu.make_async_copy(source, target, self.sems.at[self.used])
        self.used += 1
        copy.start()
        return copy

    def tiles(self, source, target, rows=None):
        rows = source.shape[0] if rows is None else rows
        return Group(
            self.start(source.at[:, columns(t)], target.at[t, pl.ds(PAD, rows), :])
            for t in range(source.shape[1] // LANES)
        )

    def untiled(self, source, target):
        rows = target.shape[0]
        return Group(
            self.start(source.at[t, pl.ds(PAD, rows), :], target.at[:, columns(t)])
            for t in range(target.shape[1] // LANES)
        )

    def choose(self, first_if, source, other, target):
        copy = pltpu.make_async_copy(source, target, self.sems.at[self.used])
        swap = pltpu.make_async_copy(other, target, self.sems.at[self.used])
        self.used += 1

        @pl.when(first_if)
        def _():
            copy.start()

        @pl.when(jnp.logical_not(first_if))
        def _():
            swap.start()

        return copy


def clear_pads(tiles, size):
    zeros = jnp.zeros(tiles.shape[:2] + (PAD, LANES), F32)
    tiles[:, :, :PAD, :] = zeros
    tiles[:, :, PAD + size :, :] = zeros


def clear_top(tiles):
    tiles[:, :, :PAD, :] = jnp.zeros(tiles.shape[:2] + (PAD, LANES), F32)


def columns(tile):
    return pl.ds(tile * LANES, LANES)


def load_rows(ref, plane, row, offset=0):
    return [ref[plane, t, pl.ds(PAD + row + offset, ROWS), :] for t in range(ref.shape[1])]


def load_flat(ref, plane, row):
    part = pl.ds(row, ROWS)
    return [ref[plane, part, columns(t)] for t in range(ref.shape[2] // LANES)]


def store_rows(ref, plane, row, values):
    for t, value in enumerate(values):
        ref[plane, t, pl.ds(PAD + row, ROWS), :] = value


def store_flat(ref, plane, row, values):
    for t, value in enumerate(values):
        ref[plane, pl.ds(row, ROWS), columns(t)] = value


def store_whole(ref, plane, row, value):
    ref[plane, pl.ds(row, ROWS), :] = value


def each(function, *lists):
    return [function(*values) for values in zip(*lists)]


def lane_sides(centre):
    lane = lax.broadcasted_iota(jnp.int32, (ROWS, LANES), 1)
    first = lane == 0
    last = lane == LANES - 1
    up = [pltpu.roll(value, 1, 1) for value in centre]
    down = [pltpu.roll(value, LANES - 1, 1) for value in centre]
    left = [jnp.where(first, up[t - 1] if t else 0.0, up[t]) for t in range(len(centre))]
    right = [
        jnp.where(last, down[t + 1] if t + 1 < len(centre) else 0.0, down[t])
        for t in range(len(centre))
    ]
    return [left, right]


def around(ref, plane, row, sides):
    centre = load_rows(ref, plane, row)
    beside = lane_sides(centre)
    beside += [load_rows(ref, plane, row, 1), load_rows(ref, plane, row, -1)]
    beside += [load_rows(ref, plane + side, row) for side in sides]
    return centre, beside


def face_totals(coef, beside):
    result = each(lambda c, s: c + s, coef, beside[0])
    for side in beside[1:]:
        result = each(lambda r, c, s: r + (c + s), result, coef, side)
    return result


def stencil(coefs, fields, row, coef_plane, field_plane, sides):
    coef, coef_beside = around(coefs, coef_plane, row, sides)
    here, beside = around(fields, field_plane, row, sides)
    weights = [each(lambda c, s: c + s, coef, side) for side in coef_beside]
    twice = weights[0]
    gathered = each(lambda w, v: w * v, weights[0], beside[0])
    for weight, side in zip(weights[1:], beside[1:]):
        twice = each(lambda a, b: a + b, twice, weight)
        gathered = each(lambda a, w, v: a + w * v, gathered, weight, side)
    return twice, gathered, here, coef


def first_of(rhs, twice):
    return each(lambda b, d: (2.0 * OMEGA) * b / d, rhs, twice)


def smoothed_of(rhs, twice, gathered, here):
    return each(
        lambda b, d, g, v: (1.0 - OMEGA) * v + ((2.0 * OMEGA) * b + OMEGA * g) / d,
        rhs, twice, gathered, here,
    )


def residual_of(rhs, twice, gathered, here):
    return each(lambda b, d, g, v: b - 0.5 * (d * v - g), rhs, twice, gathered, here)


def total(values):
    result = values[0]
    for value in values[1:]:
        result = result + value
    return result


def sweep(size, body, start=0):
    def step(index, carry):
        for store, ref, plane, row, values in body(pl.multiple_of(index * ROWS, ROWS)):
            store(ref, plane, row, values)
        return carry

    lax.fori_loop(start // ROWS, size // ROWS, step, 0, unroll=UNROLL)


def in_halves(size):
    return ((0, size // 2), (size // 2, size))


def thin_rows(tiles, plane, start, count):
    parts = []
    for tile in range(tiles.shape[1]):
        parts.append(
            0.25 * tiles[plane, tile, pl.ds(PAD - 1 + start, count, stride=2), :]
            + 0.5 * tiles[plane, tile, pl.ds(PAD + start, count, stride=2), :]
            + 0.25 * tiles[plane, tile, pl.ds(PAD + 1 + start, count, stride=2), :]
        )
    return jnp.concatenate(parts, axis=1)


def restrict_plane(tiles, plane, size, matrix):
    return project(thin_rows(tiles, plane, 0, size // 2), matrix)


def project(rows, matrix):
    high = rows.astype(BF16)
    rest = rows - high.astype(F32)
    middle = rest.astype(BF16)
    low = (rest - middle.astype(F32)).astype(BF16)
    return (
        jnp.dot(low, matrix, preferred_element_type=F32)
        + jnp.dot(middle, matrix, preferred_element_type=F32)
        + jnp.dot(high, matrix, preferred_element_type=F32)
    )


def plane_at(core, place):
    return place + core * (3 - 2 * place)


def first_inner(scalars, coef, rhs, first, partial, c, b, f, g, sems):
    core = scalars[0]
    size = coef.shape[1]
    go = Copies(sems)
    waits = [go.tiles(coef.at[plane_at(core, q)], c.at[q]) for q in (0, 1)]
    later = [[go.tiles(coef.at[plane_at(core, 2)], c.at[2])]]
    later[0].append(go.start(rhs.at[plane_at(core, 1)], b.at[0]))
    later.append([go.tiles(coef.at[plane_at(core, 3)], c.at[3])])
    later[1].append(go.start(rhs.at[plane_at(core, 2)], b.at[1]))
    clear_pads(c, size)
    for copy in waits:
        copy.wait()
    out = []

    def partial_plane(slot, q, side):
        def rows(row):
            coef_here, beside = around(c, q, row, (side,))
            twice = face_totals(coef_here, beside)
            return [(store_flat, g, slot, row, each(lambda d, v: d + v, twice, coef_here))]

        sweep(size, rows)
        out.append(go.start(g.at[slot], partial.at[slot]))

    def first_plane(q):
        def rows(row):
            twice = face_totals(*around(c, q, row, (-1, 1)))
            return [(store_flat, f, q - 1, row, first_of(load_flat(b, q - 1, row), twice))]

        sweep(size, rows)
        out.append(go.start(f.at[q - 1], first.at[q - 1]))

    partial_plane(0, 0, 1)
    for copy in later[0]:
        copy.wait()
    first_plane(1)
    for copy in later[1]:
        copy.wait()
    first_plane(2)
    partial_plane(1, 3, -1)
    for copy in out:
        copy.wait()


def first_rim(scalars, rhs, partial, coef_outer, coef_sibling, outer, sibling, b, g, h, f, sems):
    core = scalars[0]
    size = rhs.shape[1]
    go = Copies(sems)
    loads = []
    for slot, q, halo in ((1, 3, coef_sibling), (0, 0, coef_outer)):
        for start, stop in in_halves(size):
            part = pl.ds(start, stop - start)
            loads.append(
                [
                    go.start(rhs.at[plane_at(core, q), part], b.at[slot, part]),
                    go.start(partial.at[slot, part], g.at[slot, part]),
                    go.start(halo.at[part], h.at[slot, part]),
                ]
            )
    out = []
    for slot, target in ((1, sibling), (0, outer)):
        for start, stop in in_halves(size):
            for copy in loads.pop(0):
                copy.wait()

            def rows(row):
                twice = each(lambda g, h: g + h, load_flat(g, slot, row), load_flat(h, slot, row))
                return [(store_flat, f, slot, row, first_of(load_flat(b, slot, row), twice))]

            sweep(stop, rows, start)
            part = pl.ds(start, stop - start)
            out.append(go.start(f.at[slot, part], target.at[part]))
    for copy in out:
        copy.wait()


def loads_in_order(go, core, coef, rhs, coef_outer, coef_sibling, sources, c, v, b):
    def coef_in(q):
        if q == 0:
            return go.tiles(coef_outer, c.at[0])
        if q == 5:
            return go.tiles(coef_sibling, c.at[5])
        return go.tiles(coef.at[plane_at(core, q - 1)], c.at[q])

    def field_in(q):
        return go.tiles(sources[q - 1], v.at[q])

    def rhs_in(q):
        return go.start(rhs.at[plane_at(core, q - 1)], b.at[q - 1])

    waits = [[coef_in(0), coef_in(1), coef_in(2), field_in(1), field_in(2), rhs_in(1)]]
    waits.append([coef_in(3), field_in(3), rhs_in(2)])
    waits.append([coef_in(4), field_in(4), rhs_in(3)])
    waits.append([coef_in(5), rhs_in(4)])
    return waits


def smooth_inner(
    scalars, coef, rhs, coef_outer, coef_sibling, first, first_outer, first_sibling,
    smooth, known, factor, c, v, b, s, g, h, sems,
):
    core = scalars[0]
    size = coef.shape[1]
    go = Copies(sems)
    sources = (first_outer, first.at[0], first.at[1], first_sibling)
    waits = loads_in_order(go, core, coef, rhs, coef_outer, coef_sibling, sources, c, v, b)
    clear_pads(c, size)
    clear_pads(v, size)
    out = []

    def rim(slot, q, side):
        def rows(row):
            twice, gathered, here, coef_here = stencil(c, v, row, q, q, (side,))
            edge = each(lambda c, h: c + h, coef_here, load_rows(c, q - side, row))
            twice = each(lambda d, e: d + e, twice, edge)
            scale = [1.0 / value for value in twice]
            known_rows = each(
                lambda b, d, g, v: (1.0 - OMEGA) * v + ((2.0 * OMEGA) * b + OMEGA * g) * d,
                load_flat(b, q - 1, row), scale, gathered, here,
            )
            factor_rows = each(lambda d, e: (OMEGA * e) * d, scale, edge)
            return [(store_flat, g, slot, row, known_rows), (store_flat, h, slot, row, factor_rows)]

        sweep(size, rows)
        out.append(go.start(g.at[slot], known.at[slot]))
        out.append(go.start(h.at[slot], factor.at[slot]))

    def middle(q):
        def rows(row):
            twice, gathered, here, _ = stencil(c, v, row, q, q, (-1, 1))
            values = smoothed_of(load_flat(b, q - 1, row), twice, gathered, here)
            return [(store_flat, s, q - 2, row, values)]

        sweep(size, rows)
        out.append(go.start(s.at[q - 2], smooth.at[plane_at(core, q - 1)]))

    steps = ((rim, (0, 1, 1)), (middle, (2,)), (middle, (3,)), (rim, (1, 4, -1)))
    for needed, (work, arguments) in zip(waits, steps):
        for copy in needed:
            copy.wait()
        work(*arguments)
    for copy in out:
        copy.wait()


def rim_loads(go, known, factor, halo_outer, halo_sibling, g, h, v):
    loads = []
    for slot, halo in ((1, halo_sibling), (0, halo_outer)):
        for start, stop in in_halves(known.shape[1]):
            part = pl.ds(start, stop - start)
            loads.append(
                [
                    go.start(known.at[slot, part], g.at[slot, part]),
                    go.start(factor.at[slot, part], h.at[slot, part]),
                    go.start(halo.at[part], v.at[slot, part]),
                ]
            )
    return loads


def smooth_rim(
    scalars, started, known, factor, halo_outer, halo_sibling,
    smooth, outer, sibling, g, h, v, s, sems,
):
    core = scalars[0]
    size = known.shape[1]
    go = Copies(sems)
    loads = rim_loads(go, known, factor, halo_outer, halo_sibling, g, h, v)
    out = []
    for slot, q, target in ((1, 3, sibling), (0, 0, outer)):
        for start, stop in in_halves(size):
            for copy in loads.pop(0):
                copy.wait()

            def rows(row):
                flat = [load_flat(ref, slot, row) for ref in (g, h, v)]
                return [(store_flat, s, slot, row, each(lambda g, h, v: g + h * v, *flat))]

            sweep(stop, rows, start)
            part = pl.ds(start, stop - start)
            out.append(go.start(s.at[slot, part], target.at[part]))
            out.append(go.start(s.at[slot, part], smooth.at[plane_at(core, q), part]))
    for copy in out:
        copy.wait()


def residual_inner(
    scalars, coef, rhs, coef_outer, coef_sibling, smooth, smooth_outer, smooth_sibling, matrix,
    lowered, known, factor, c, v, b, g, h, t, low, mat, sems,
):
    core = scalars[0]
    size = coef.shape[1]
    go = Copies(sems)
    sources = (
        smooth_outer, smooth.at[plane_at(core, 1)], smooth.at[plane_at(core, 2)], smooth_sibling,
    )
    waits = loads_in_order(go, core, coef, rhs, coef_outer, coef_sibling, sources, c, v, b)
    waits[0].append(go.start(matrix, mat))
    clear_pads(c, size)
    clear_pads(v, size)
    clear_top(t)
    out = []

    def rim(slot, q, side):
        def rows(row):
            twice, gathered, here, coef_here = stencil(c, v, row, q, q, (side,))
            edge = each(lambda c, h: c + h, coef_here, load_rows(c, q - side, row))
            twice = each(lambda d, e: d + e, twice, edge)
            known_rows = residual_of(load_flat(b, q - 1, row), twice, gathered, here)
            factor_rows = [0.5 * value for value in edge]
            return [(store_flat, g, slot, row, known_rows), (store_flat, h, slot, row, factor_rows)]

        sweep(size, rows)
        out.append(go.start(g.at[slot], known.at[slot]))
        out.append(go.start(h.at[slot], factor.at[slot]))

    def middle(q):
        def rows(row):
            twice, gathered, here, _ = stencil(c, v, row, q, q, (-1, 1))
            values = residual_of(load_flat(b, q - 1, row), twice, gathered, here)
            return [(store_rows, t, q - 2, row, values)]

        sweep(size, rows)
        low[q - 2] = restrict_plane(t, q - 2, size, mat[...])

    steps = ((rim, (0, 1, 1)), (middle, (2,)), (middle, (3,)), (rim, (1, 4, -1)))
    for needed, (work, arguments) in zip(waits, steps):
        for copy in needed:
            copy.wait()
        work(*arguments)
    out.append(go.start(low, lowered))
    for copy in out:
        copy.wait()


def residual_rim(
    scalars, known, factor, halo_outer, halo_sibling, lowered, matrix,
    packed, g, h, v, t, low, pack, mat, sems,
):
    core = scalars[0]
    size = known.shape[1]
    go = Copies(sems)
    more = [go.start(lowered, low.at[pl.ds(1, 2)]), go.start(matrix, mat)]
    loads = rim_loads(go, known, factor, halo_outer, halo_sibling, g, h, v)
    clear_top(t)
    for copy in more:
        copy.wait()
    for slot in (1, 0):
        for start, stop in in_halves(size):
            for copy in loads.pop(0):
                copy.wait()

            def rows(row):
                flat = [load_flat(ref, slot, row) for ref in (g, h, v)]
                return [(store_rows, t, slot, row, each(lambda g, h, v: g + h * v, *flat))]

            sweep(stop, rows, start)
        low[3 * slot] = restrict_plane(t, slot, size, mat[...])
    one = plane_at(core, 1)
    two = plane_at(core, 2)
    last = low[plane_at(core, 3)]
    pack[0] = 2.0 * low[plane_at(core, 0)] + low[one]
    pack[1] = low[one] + 2.0 * low[two] + last
    pack[2] = last
    copy = go.start(pack, packed)
    copy.wait()


def guarded(values):
    return [jnp.where(value == 0.0, 1.0, value) for value in values]


def first_wide(c, b, f, planes, size):
    def plane(q):
        def rows(row):
            twice = guarded(face_totals(*around(c, q + 1, row, (-1, 1))))
            return [(store_rows, f, q, row, first_of(load_flat(b, q, row), twice))]

        sweep(size, rows)

    pl.loop(0, planes)(plane)


def smooth_wide(c, b, f, s, planes, size, inside):
    def plane(q):
        keep = inside(q)

        def rows(row):
            twice, gathered, here, _ = stencil(c, f, row, q + 2, q + 1, (-1, 1))
            values = smoothed_of(load_flat(b, q + 1, row), guarded(twice), gathered, here)
            return [(store_rows, s, q, row, [jnp.where(keep, value, 0.0) for value in values])]

        sweep(size, rows)

    pl.loop(0, planes)(plane)


def residual_wide(c, b, s, t, planes, size):
    for q in range(planes):

        def rows(row):
            twice, gathered, here, _ = stencil(c, s, row, q + 3, q + 1, (-1, 1))
            values = residual_of(load_flat(b, q + 2, row), twice, gathered, here)
            return [(store_rows, t, q, row, values)]

        sweep(size, rows)


def middle_level(
    scalars, own, sibling, outer, rim_outer, rim_sibling, coef, coef_sibling, coef_outer,
    coef_beyond, matrix, smooth, packed, m, b, c, f, s, t, pack, mat, sems,
):
    core = scalars[0]
    place = scalars[1]
    final = scalars[2]
    size = coef.shape[1]
    even = core == 0
    go = Copies(sems)
    three = pl.ds(0, 3)
    loads = [
        go.start(own, m.at[pl.ds(3, 3)]),
        go.choose(even, outer, sibling, m.at[three]),
        go.choose(even, sibling, outer, m.at[pl.ds(6, 3)]),
        go.choose(even, rim_outer, rim_sibling, m.at[9]),
        go.start(matrix, mat),
    ]
    for tile in range(size // LANES):
        part = columns(tile)
        for q in range(2):
            left = c.at[1 + q, tile, pl.ds(PAD, size), :]
            right = c.at[5 + q, tile, pl.ds(PAD, size), :]
            loads.append(go.choose(even, coef_outer.at[q, :, part], coef_sibling.at[q, :, part], left))
            loads.append(go.choose(even, coef_sibling.at[q, :, part], coef_outer.at[q, :, part], right))
        left = c.at[0, tile, pl.ds(PAD, size), :]
        right = c.at[7, tile, pl.ds(PAD, size), :]
        loads.append(go.choose(even, coef_outer.at[2, :, part], coef_beyond.at[:, part], left))
        loads.append(go.choose(even, coef_beyond.at[:, part], coef_outer.at[2, :, part], right))
    loads += [go.tiles(coef.at[q], c.at[3 + q]) for q in range(2)]
    clear_pads(c, size)
    clear_pads(f, size)
    clear_pads(s, size)
    clear_top(t)
    for copy in loads:
        copy.wait()

    def rows(row):
        part = pl.ds(row, ROWS)
        values = [
            m[0, part, :] + m[9, part, :],
            m[1, part, :],
            m[3, part, :] + m[2, part, :],
            m[4, part, :],
            jnp.where(place < final, m[6, part, :] + m[5, part, :], 0.0),
            m[7, part, :],
        ]
        return [(store_whole, b, q, row, value) for q, value in enumerate(values)]

    sweep(size, rows)
    first_wide(c, b, f, 6, size)
    lowest = jnp.where(place > 0, 0, 1)
    highest = jnp.where(place < final, 3, 2)
    smooth_wide(c, b, f, s, 4, size, lambda q: jnp.logical_and(q >= lowest, q <= highest))
    out = [go.untiled(s.at[1 + q], smooth.at[q]) for q in range(2)]
    residual_wide(c, b, s, t, 2, size)
    low = restrict_plane(t, 1, size, mat[...])
    pack[0] = 2.0 * restrict_plane(t, 0, size, mat[...]) + low
    pack[1] = low
    out.append(go.start(pack, packed))
    for copy in out:
        copy.wait()


def last_level(
    scalars, own, sibling, even_chip, odd_chip, even_beside, odd_beside, third, matrices,
    smooth, copies, n, b, c, f, s, t, w, mat, sems,
):
    core = scalars[0]
    place = scalars[1]
    final = scalars[2]
    size = own.shape[1]
    half = size // 2
    left_core = core == 0
    left_is_odd = (place // 2) % 2 == 0
    go = Copies(sems)
    nearer = [
        go.start(own, n.at[3]),
        go.start(sibling, n.at[jnp.where(left_core, 4, 2)]),
        go.choose(left_is_odd, odd_chip, even_chip, n.at[1]),
        go.choose(left_is_odd, even_chip, odd_chip, n.at[5]),
        go.choose(left_is_odd, odd_beside, even_beside, n.at[jnp.where(left_core, 2, 0)]),
        go.choose(left_is_odd, even_beside, odd_beside, n.at[jnp.where(left_core, 6, 4)]),
        go.start(third, n.at[jnp.where(left_core, 0, 6), pl.ds(1, 2)]),
        go.start(matrices, mat),
    ]
    clear_pads(c, size)
    clear_pads(f, size)
    clear_pads(s, size)
    clear_top(t)
    for copy in nearer:
        copy.wait()

    def coef_rows(row):
        return [(store_rows, c, q, row, [n[q, 2, pl.ds(row, ROWS), :]]) for q in range(7)]

    sweep(size, coef_rows)

    def rows(row):
        part = pl.ds(row, ROWS)
        values = [
            n[1, 0, part, :] + n[0, 1, part, :],
            n[2, 0, part, :] + n[1, 1, part, :],
            n[3, 0, part, :] + n[2, 1, part, :],
            jnp.where(place < final, n[4, 0, part, :] + n[3, 1, part, :], 0.0),
            jnp.where(place < final - 1, n[5, 0, part, :] + n[4, 1, part, :], 0.0),
        ]
        return [(store_whole, b, q, row, value) for q, value in enumerate(values)]

    sweep(size, rows)
    first_wide(c, b, f, 5, size)
    lowest = jnp.where(place > 0, 0, 1)
    highest = jnp.where(place < final, 2, 1)
    smooth_wide(c, b, f, s, 3, size, lambda q: jnp.logical_and(q >= lowest, q <= highest))
    out = [go.untiled(s.at[1], smooth.at[0])]
    residual_wide(c, b, s, t, 1, size)
    top = thin_rows(t, 0, 0, size // 4)
    bottom = thin_rows(t, 0, half, size // 4)
    result = project(top, mat[0]) + project(bottom, mat[1])
    w[...] = jnp.broadcast_to(result[None], w.shape)
    out.append(go.start(w, copies))
    for copy in out:
        copy.wait()


def coarse_level(scalars, own, sibling, coef, solution, e, o, c, w, p0, p1, g, y, sems):
    core = scalars[0]
    even = core == 0
    half, size, lanes = coef.shape
    go = Copies(sems)
    loads = [
        go.start(coef, c.at[pl.ds(1, half)]),
        go.choose(even, own, sibling, e),
        go.choose(even, sibling, own, o.at[pl.ds(1, 2 * half)]),
    ]
    o[0] = jnp.zeros(o.shape[1:], F32)
    loads[0].wait()
    lane = lax.broadcasted_iota(jnp.int32, (size, lanes), 1)
    row = lax.broadcasted_iota(jnp.int32, (size, lanes), 0)
    upper = lane >= size
    low_edge = (lane % size) == 0
    high_edge = (lane % size) == size - 1
    c[0] = jnp.where(upper, pltpu.roll(c[half], size, 1), 0.0)
    c[half + 1] = jnp.where(upper, 0.0, pltpu.roll(c[1], size, 1))

    edges = [row == size - 1, row == 0, high_edge, low_edge]
    for copy in loads[1:]:
        copy.wait()
    short = lax.broadcasted_iota(jnp.int32, (size // 2, lanes), 1) >= size

    def prepare(q, carry):
        here = c[q + 1]
        sides = [
            pltpu.roll(here, size - 1, 0), pltpu.roll(here, 1, 0),
            pltpu.roll(here, lanes - 1, 1), pltpu.roll(here, 1, 1),
        ]
        sides = [jnp.where(edge, 0.0, value) for edge, value in zip(edges, sides)]
        sides += [c[q], c[q + 2]]
        inverse = 1.0 / (3.0 * here + 0.5 * total(sides))
        scaled = 0.5 * inverse
        for d, side in enumerate(sides):
            weight = (here + side) * scaled
            if d < 4:
                weight = jnp.where(edges[d], 0.0, weight)
            elif d == 4:
                weight = jnp.where(jnp.logical_and(q == 0, jnp.logical_not(upper)), 0.0, weight)
            else:
                weight = jnp.where(jnp.logical_and(q == half - 1, upper), 0.0, weight)
            w[d, q] = weight
        lower_rhs = o[q] + 2.0 * e[q] + o[q + 1]
        upper_rhs = o[q + half] + 2.0 * e[q + half] + o[q + half + 1]
        top = jnp.where(short, pltpu.roll(upper_rhs, size, 1), lower_rhs)
        bottom = jnp.where(short, upper_rhs, pltpu.roll(lower_rhs, size, 1))
        scaled_rhs = jnp.concatenate([top, bottom], axis=0) * inverse
        g[q] = scaled_rhs
        p1[q + 1, PAD : PAD + size] = scaled_rhs * (1.0 / CENTER_VALUE)
        p0[q + 1, PAD : PAD + size] = jnp.zeros((size, lanes), F32)
        return carry

    zeros = jnp.zeros((half + 2, PAD, lanes), F32)
    for p in (p0, p1):
        p[:, :PAD] = zeros
        p[:, PAD + size :] = zeros
    lax.fori_loop(0, half, prepare, 0, unroll=4)
    sigma = CENTER_VALUE / HALF_WIDTH
    rho = 1.0 / sigma
    block = pl.ds(PAD, size)
    for index in range(CHEB - 1):
        older, now = (p0, p1) if index % 2 == 0 else (p1, p0)
        now[0, block] = pltpu.roll(now[half, block], size, 1)
        now[half + 1, block] = pltpu.roll(now[1, block], size, 1)
        rho_new = 1.0 / (2.0 * sigma - rho)
        keep = rho_new * rho
        gain = 2.0 * rho_new / HALF_WIDTH
        rho = rho_new
        final = index == CHEB - 2

        def advance(q, carry):
            values = []
            for start in range(0, size, ROWS):
                part = pl.ds(PAD + start, ROWS)
                flat = pl.ds(start, ROWS)
                here = now[q + 1, part]
                sides = [
                    now[q + 1, pl.ds(PAD + start + 1, ROWS)],
                    now[q + 1, pl.ds(PAD + start - 1, ROWS)],
                    pltpu.roll(here, lanes - 1, 1), pltpu.roll(here, 1, 1),
                    now[q, part], now[q + 2, part],
                ]
                near = total([w[d, q, flat] * side for d, side in enumerate(sides)])
                remains = (g[q, flat] - here) + near
                values.append(here + keep * (here - older[q + 1, part]) + gain * remains)
            for index, value in enumerate(values):
                start = index * ROWS
                if final:
                    flat = pl.ds(start, ROWS)
                    y[q, flat] = value[:, :size]
                    y[q + half, flat] = pltpu.roll(value, size, 1)[:, :size]
                else:
                    older[q + 1, pl.ds(PAD + start, ROWS)] = value
            return carry

        lax.fori_loop(0, half, advance, 0, unroll=2 * UNROLL)
    copy = go.start(y, solution)
    copy.wait()


def vm(*dims):
    return pltpu.VMEM(dims, F32)


def tiled(planes, size):
    return vm(planes, size // LANES, size + 2 * PAD, LANES)


def swapped(value, pairs):
    return lax.ppermute(value, "box", pairs)


def local(rhs_fine, coef_zero, coef_one, coef_two, coef_three):
    count = lax.axis_size("box")
    place = lax.axis_index("box")
    core = place % 2
    scalars = jnp.stack([core, place, jnp.int32(count - 1)]).astype(jnp.int32)
    near = [(i, i ^ 1) for i in range(count)]
    far = [(i, i + 1) for i in range(1, count - 1, 2)]
    far = far + [(j, i) for i, j in far]

    n = coef_zero.shape[1]
    n1, n2 = n // 2, n // 4
    n3 = n // 8
    plane = n * n * 4
    matrix0 = jnp.asarray(restriction_matrix(n, n1, 0), BF16)
    matrix1 = jnp.asarray(restriction_matrix(n1, n2, 0), BF16)
    both = np.stack([restriction_matrix(n2, 2 * n3, 0), restriction_matrix(n2, 2 * n3, n3)])
    matrix2 = jnp.asarray(both, BF16)

    def side_plane(field, where):
        return lax.dynamic_index_in_dim(field, where, 0, keepdims=False)

    coef_outer = swapped(side_plane(coef_zero, 3 * core), far)
    coef_sibling = swapped(side_plane(coef_zero, 3 - 3 * core), near)
    first, partial = call(
        first_inner, [shape(2, n, n), shape(2, n, n)],
        [tiled(4, n), vm(2, n, n), vm(2, n, n), vm(2, n, n)], 24, 40 * n * n, 12 * plane, 32,
    )(scalars, coef_zero, rhs_fine)
    coefs_sibling = swapped(coef_one, near)
    beyond = lax.dynamic_slice_in_dim(coefs_sibling, core, 1, 0)
    coefs_out = jnp.concatenate([coef_one, beyond], axis=0)
    partial, coefs_out = lax.optimization_barrier((partial, coefs_out))
    first_outer, first_sibling = call(
        first_rim, [shape(n, n), shape(n, n)],
        [vm(2, n, n)] * 4, 16, 10 * n * n, 8 * plane, 32,
    )(scalars, rhs_fine, partial, coef_outer, coef_sibling)

    halo_outer = swapped(first_outer, far)
    halo_sibling = swapped(first_sibling, near)
    smooth, known, factor = call(
        smooth_inner, [shape(4, n, n), shape(2, n, n), shape(2, n, n)],
        [tiled(6, n), tiled(6, n), vm(4, n, n), vm(2, n, n), vm(2, n, n), vm(2, n, n)],
        54, 160 * n * n, 20 * plane, 62,
    )(scalars, coef_zero, rhs_fine, coef_outer, coef_sibling, first, first_outer, first_sibling)
    coefs_out, known = lax.optimization_barrier((coefs_out, known))
    coefs_outer = swapped(coefs_out, far)
    smooth_zero, smooth_outer, smooth_sibling = call(
        smooth_rim, [shape(4, n, n), shape(n, n), shape(n, n)],
        [vm(2, n, n)] * 4, 20, 4 * n * n, 10 * plane, 62, {1: 0},
    )(scalars, smooth, known, factor, halo_outer, halo_sibling)

    halo_outer = swapped(smooth_outer, far)
    halo_sibling = swapped(smooth_sibling, near)

    smooth_outer, coefs_outer = lax.optimization_barrier((smooth_outer, coefs_outer))
    lowered, known, factor = call(
        residual_inner, [shape(2, n1, n1), shape(2, n, n), shape(2, n, n)],
        [tiled(6, n), tiled(6, n), vm(4, n, n), vm(2, n, n), vm(2, n, n),
         tiled(2, n), vm(2, n1, n1), pltpu.VMEM((n, n1), BF16)],
        54, 160 * n * n, 20 * plane, 62,
    )(scalars, coef_zero, rhs_fine, coef_outer, coef_sibling, smooth_zero, smooth_outer,
      smooth_sibling, matrix0)
    coefs_beyond = swapped(lax.dynamic_index_in_dim(coefs_outer, 1 - core, 0, False), near)
    lowered, coefs_beyond = lax.optimization_barrier((lowered, coefs_beyond))
    (packed,) = call(
        residual_rim, [shape(3, n1, n1)],
        [vm(2, n, n), vm(2, n, n), vm(2, n, n), tiled(2, n), vm(4, n1, n1), vm(3, n1, n1),
         pltpu.VMEM((n, n1), BF16)],
        15, 20 * n * n, 8 * plane, 62,
    )(scalars, known, factor, halo_outer, halo_sibling, lowered, matrix0)

    packed_outer = swapped(packed, far)
    packed_sibling = swapped(packed, near)
    rim_outer = swapped(packed_sibling[2], far)
    rim_sibling = swapped(packed_outer[2], near)
    smooth_one, packed = call(
        middle_level, [shape(2, n1, n1), shape(2, n2, n2)],
        [vm(10, n1, n1), vm(6, n1, n1), tiled(8, n1), tiled(6, n1),
         tiled(4, n1), tiled(2, n1), vm(2, n2, n2), pltpu.VMEM((n1, n2), BF16)],
        40, 400 * n1 * n1, 24 * n1 * n1 * 4, 40,
    )(scalars, packed, packed_sibling, packed_outer, rim_outer, rim_sibling, coef_one,
      coefs_sibling, coefs_outer, coefs_beyond, matrix1)

    chip_even = [(i, i ^ 2) for i in range(count)]
    chip_odd = [(i, i + 2) for i in range(count - 2) if i & 2]
    chip_odd = chip_odd + [(j, i) for i, j in chip_odd]
    third = [(i, i + 3) for i in range(1, count - 3, 2)]
    third = third + [(j, i) for i, j in third]
    sent = jnp.concatenate([packed, coef_two], axis=0)
    even_chip = swapped(sent, chip_even)
    odd_chip = swapped(sent, chip_odd)
    packed_third = swapped(sent[1:], third)
    packed_sibling = swapped(sent, near)
    even_chip, odd_chip, packed_third = lax.optimization_barrier(
        (even_chip, odd_chip, packed_third)
    )
    even_beside = swapped(even_chip, near)
    odd_beside = swapped(odd_chip, near)
    groups = [[i for i in range(count) if i % 2 == r] for r in range(2)]
    smooth_two, copies = call(
        last_level, [shape(1, n2, n2), shape(count // 2, n3 // 2, 2 * n3)],
        [vm(7, 3, n2, n2), vm(5, n2, n2), tiled(7, n2), tiled(5, n2),
         tiled(3, n2), tiled(1, n2), vm(count // 2, n3 // 2, 2 * n3),
         pltpu.VMEM((2, n2, 2 * n3), BF16)],
        24, 300 * n2 * n2, 40 * n2 * n2 * 4, 40,
    )(scalars, sent, packed_sibling, even_chip, odd_chip, even_beside, odd_beside, packed_third,
      matrix2)

    gathered = lax.all_to_all(copies, "box", 0, 0, tiled=True, axis_index_groups=groups)
    gathered_sibling = swapped(gathered, near)
    half = n3 // 2
    coef_pair = jnp.concatenate([coef_three[:half], coef_three[half:]], axis=2)
    (coarse_solution,) = call(
        coarse_level, [shape(n3, n3, n3)],
        [vm(n3, half, 2 * n3), vm(n3 + 1, half, 2 * n3), vm(half + 2, n3, 2 * n3),
         vm(6, half, n3, 2 * n3), vm(half + 2, n3 + 16, 2 * n3), vm(half + 2, n3 + 16, 2 * n3), vm(half, n3, 2 * n3),
         vm(n3, n3, n3)],
        4, 300 * n3 * n3 * n3, 20 * n3 * n3 * n3, 48,
    )(scalars, gathered, gathered_sibling, coef_pair)
    return (smooth_zero, smooth_one, smooth_two, coarse_solution)


def solution(mesh):
    placed = (
        P("box", None, None),
        P("box", None, None),
        P("box", None, None),
        P("box", None, None),
        P(),
    )
    return jax.shard_map(
        local,
        mesh=mesh,
        in_specs=placed,
        out_specs=(P("box", None, None), P("box", None, None), P("box", None, None), P()),
        check_vma=False,
    )
```
